512 devices in a mesh: ctx: 32 (over z_hi, y, core), tp: 16 (over z_lo, x).
Axes of the slice: x: 4, y: 4, z: 16 (z_hi: 4, z_lo: 4; z = z_hi * 4 + z_lo), core: 2. Of those that a mesh axis runs over, the one named last changes fastest.
Arguments:
- lin_q: bfloat16 [64, 8192, 128], P('tp', 'ctx'), may hold values from -6 to 6
- lin_k: bfloat16 [64, 8192, 128], P('tp', 'ctx'), may hold values from -0.5 to 0.5
- lin_v: bfloat16 [64, 8192, 128], P('tp', 'ctx'), may hold values from -6 to 6
- log_decay: float32 [64, 8192], P('tp', 'ctx'), may hold values from -1 to 0
- prior_state: float32 [64, 128, 128], P('tp'), may hold values from -48 to 48
- lin_gain: float32 [64, 128], P('tp'), may hold values from 0.5 to 1.5
- soft_q: bfloat16 [64, 8192, 128], P('tp', 'ctx'), may hold values from -23 to 23
- span_k: bfloat16 [8, 8192, 128], P(None, 'ctx'), may hold values from -4 to 4
- span_v: bfloat16 [8, 8192, 128], P(None, 'ctx'), may hold values from -6 to 6
- cache_k: bfloat16 [8, 4096, 128], P(None, 'ctx'), may hold values from -4 to 4
- cached_value_rows: bfloat16 [8, 4096, 128], P(None, 'ctx'), may hold values from -6 to 6
- cache_len: int32 [32], replicated, may hold values from 2 to 128, as said below
Outputs:
- lightning_normalized_result: bfloat16 [64, 8192, 128], P('tp', 'ctx')
- soft_out: bfloat16 [64, 8192, 128], P('tp', 'ctx')
The draws below stay inside these ranges and needn't reach their ends.
Inputs may be any that keep to these rules, and one draw needn't show every extreme that they name: Block r holds cache_len[r] live rows from its start; some block is full in every draw.
All inputs are finite; a program needn't handle non-finite values.
Results may differ from the reference program's by a relative error of at most 0.01.
Values may be sent and summed in bfloat16 or wider, within the bound.
No kernel may reach another device: no remote copies, remote signals or barrier semaphores. Data moves between devices by JAX's collectives and lax.ppermute only.
A program may use at most 64 MiB of HBM per device.

```python
import math
import jax
import jax.numpy as jnp
from jax import lax

HD = 128
GROUP_Q = 8
BLOCK = 256
C_DEV = 128
HEADS = 64
KVH = 8
TOKENS = 8192
CACHE = 4096
N_CTX = 32


def draw_cache_k(key, part):
    normal_key = jax.random.fold_in(key, 13)
    drawn = jnp.clip(jax.random.normal(normal_key, (KVH, CACHE, HD), jnp.float32), -4.0, 4.0)
    return drawn.astype(jnp.bfloat16)


def draw_soft_q(key, part):
    first_key = jax.random.fold_in(jax.random.fold_in(key, 23), 0)
    drawn = jnp.clip(jax.random.normal(first_key, (HEADS, TOKENS, HD), jnp.float32), -4.0, 4.0)
    return drawn.astype(jnp.bfloat16)


def draw_cache_len(key, part):
    blocks = CACHE // C_DEV
    first_key, second_key = jax.random.split(jax.random.fold_in(key, 31))
    lengths = jax.random.randint(first_key, (blocks,), 2, C_DEV + 1)
    full_block = jax.random.randint(second_key, (), 0, blocks)
    return jnp.where(jnp.arange(blocks) == full_block, C_DEV, lengths).astype(jnp.int32)


def draw_log_decay(key, part):
    keys_all = jax.random.split(jax.random.fold_in(key, 47), 7)
    fast_share = 0.5
    fast = jax.random.uniform(keys_all[0], (HEADS, 1)) < fast_share
    fast_rate = jnp.exp(jax.random.uniform(keys_all[1], (HEADS, 1), minval=math.log(1.0 / 50.0), maxval=math.log(1.0 / 30.0)))
    slow_rate = jnp.exp(jax.random.uniform(keys_all[2], (HEADS, 1), minval=math.log(0.25), maxval=math.log(1.0))) / BLOCK
    jitter = jax.random.uniform(keys_all[3], (HEADS, TOKENS), minval=0.7, maxval=1.4)
    forgetting_speed = jnp.where(fast, fast_rate, slow_rate) * jitter
    first_spot = jax.random.randint(keys_all[4], (HEADS, 1), 0, TOKENS)
    spot_step = jax.random.randint(keys_all[6], (HEADS, 1), 1, TOKENS)
    spots = jnp.concatenate([first_spot, (first_spot + spot_step) % TOKENS], axis=1)
    retention_indicator = jax.random.uniform(keys_all[5], (HEADS, 2), minval=0.5, maxval=0.8)
    agreeing_tally = jnp.arange(TOKENS)[None, None, :] == spots[:, :, None]
    contiguous_span_size = jnp.sum(jnp.where(agreeing_tally, jnp.log(retention_indicator)[:, :, None], 0.0), axis=1)
    return (contiguous_span_size - forgetting_speed).astype(jnp.float32)


def block_levels(own_key, shape, cuts, low, top_value):
    loudness = 1.0
    for dim, parts in cuts:
        steps = jax.random.uniform(jax.random.fold_in(jax.random.fold_in(own_key, 6), dim), (parts,), jnp.float32, low / len(cuts), top_value / len(cuts))
        loudness = loudness * jnp.repeat(jnp.exp(steps), shape[dim] // parts).reshape((-1,) + (1,) * (len(shape) - 1 - dim))
    return loudness


def scatter_about(own_key, shape, spread, bound, pieces=(), kind=jnp.bfloat16):
    entries = spread * jax.random.normal(own_key, shape, jnp.float32)
    if pieces:
        entries = entries * block_levels(own_key, shape, pieces, -0.22, 0.18)
    return jnp.clip(entries, -bound, bound).astype(kind)


def setup_inputs(seed: int = 0) -> dict:
    seeds = jax.random.split(jax.random.key(seed), 13)
    lin_q = scatter_about(seeds[0], (HEADS, TOKENS, HD), 1.0, 6.0, ((0, 16), (1, 32)))
    lin_k = scatter_about(seeds[1], (HEADS, TOKENS, HD), HD ** -0.5, 0.5, ((0, 16), (1, 32)))
    lin_v = scatter_about(seeds[2], (HEADS, TOKENS, HD), 1.0, 6.0, ((0, 16), (1, 32)))
    log_decay = draw_log_decay(jax.random.fold_in(seeds[12], 71), 0)
    prior_state = scatter_about(seeds[4], (HEADS, HD, HD), 8.0, 48.0, ((0, 16),), jnp.float32)
    lin_gain = jnp.clip(1.0 + 0.1 * jax.random.normal(seeds[5], (HEADS, HD), jnp.float32), 0.5, 1.5)
    soft_q = draw_soft_q(jax.random.fold_in(seeds[12], 71), 0)
    span_k = scatter_about(seeds[7], (KVH, TOKENS, HD), 1.0, 4.0, ((1, 32),))
    span_v = scatter_about(seeds[8], (KVH, TOKENS, HD), 1.0, 6.0, ((1, 32),))
    cache_k = draw_cache_k(jax.random.fold_in(seeds[12], 71), 0)
    cached_value_rows = scatter_about(seeds[10], (KVH, CACHE, HD), 1.0, 6.0, ((1, 32),))
    cache_len = draw_cache_len(jax.random.fold_in(seeds[12], 71), 0)
    return dict(lin_q=lin_q, lin_k=lin_k, lin_v=lin_v, log_decay=log_decay, prior_state=prior_state, lin_gain=lin_gain, soft_q=soft_q, span_k=span_k, span_v=span_v, cache_k=cache_k, cached_value_rows=cached_value_rows, cache_len=cache_len)


MASK_FILL = -1e+30
HIGHEST_PRECISION = lax.Precision.HIGHEST

def full_norm(value_matrix, gain_row):
    mean_square = lax.optimization_barrier(jnp.mean(value_matrix * value_matrix, axis=(0, 2), keepdims=True))
    return (value_matrix * lax.rsqrt(mean_square + 1e-05) * gain_row[:, None, :]).astype(jnp.bfloat16)

def split_blocks(array):
    shaped = array.reshape((array.shape[0], array.shape[1] // BLOCK, BLOCK) + array.shape[2:])
    return jnp.moveaxis(shaped, 1, 0)

def lightning(lin_q, lin_k, lin_v, log_decay, prior_state):
    offsets = jnp.arange(BLOCK, dtype=jnp.int32)
    causal = (offsets[:, None] >= offsets[None, :])[None]

    def block_step(state_now, inputs):
        query_part, key_part, value_part, decay_part = inputs
        cumulative = jnp.cumsum(decay_part, axis=1)
        final_sum = cumulative[:, -1:]
        decay_gap = jnp.where(causal, cumulative[:, :, None] - cumulative[:, None, :], 0.0)
        query_wide = query_part.astype(jnp.float32)
        value_wide = value_part.astype(jnp.float32)
        scores = jnp.einsum('hqd,hkd->hqk', query_wide, key_part.astype(jnp.float32))
        weights = jnp.where(causal, scores * jnp.exp(decay_gap), 0.0).astype(jnp.bfloat16)
        intra_part = jnp.einsum('hqk,hkd->hqd', weights.astype(jnp.float32), value_wide)
        inter_part = jnp.exp(cumulative)[:, :, None] * jnp.einsum('hqd,hde->hqe', query_wide, state_now, precision=HIGHEST_PRECISION)
        keyed_rows = key_part.astype(jnp.float32) * jnp.exp(final_sum - cumulative)[:, :, None]
        state_next = jnp.exp(final_sum)[:, :, None] * state_now + jnp.einsum('hkd,hke->hde', keyed_rows, value_wide, precision=HIGHEST_PRECISION)
        return (state_next, intra_part + inter_part)
    inputs = (split_blocks(lin_q), split_blocks(lin_k), split_blocks(lin_v), split_blocks(log_decay))
    final_state, mixed_blocks = lax.scan(block_step, prior_state, inputs)
    moved = jnp.moveaxis(mixed_blocks, 0, 1)
    return moved.reshape(HEADS, TOKENS, HD)

def softmax_attention(soft_q, span_k, span_v, cache_k, cached_value_rows, cache_len):
    logit_scale = 1.0 / math.sqrt(HD)
    cache_rows = jnp.arange(CACHE, dtype=jnp.int32)
    block_ids = cache_rows // C_DEV
    block_order = jnp.arange(N_CTX, dtype=jnp.int32)
    live_lengths = lax.optimization_barrier(jnp.sum(jnp.where(block_ids[:, None] == block_order[None, :], cache_len[None, :], 0), axis=1))
    cache_live = cache_rows - block_ids * C_DEV < live_lengths
    query_rows = math.gcd(TOKENS, 1024)
    head_ids = jnp.arange(HEADS, dtype=jnp.int32)
    outputs = []
    for block_index in range(TOKENS // query_rows):
        first_row = block_index * query_rows
        key_end = first_row + query_rows
        key_rows = jnp.concatenate([cache_k, span_k[:, :key_end]], axis=1)
        value_rows = jnp.concatenate([cached_value_rows, span_v[:, :key_end]], axis=1)
        query_pos = first_row + jnp.arange(query_rows, dtype=jnp.int32)
        span_live = jnp.arange(key_end, dtype=jnp.int32)[None, :] <= query_pos[:, None]
        live_mask = jnp.concatenate([jnp.broadcast_to(cache_live[None, :], (query_rows, CACHE)), span_live], axis=1)

        def per_head(inputs):
            queries, head_index = inputs
            kv_head = head_index // GROUP_Q
            head_keys = lax.dynamic_index_in_dim(key_rows, kv_head, 0, keepdims=False)
            head_values = lax.dynamic_index_in_dim(value_rows, kv_head, 0, keepdims=False)
            scores = jnp.dot(queries, head_keys.T, preferred_element_type=jnp.float32) * logit_scale
            scores = jnp.where(live_mask, scores, MASK_FILL)
            row_peak = lax.optimization_barrier(jnp.max(scores, axis=1, keepdims=True))
            probabilities = jnp.where(live_mask, jnp.exp(scores - row_peak), 0.0)
            denominator = lax.optimization_barrier(jnp.sum(probabilities, axis=1, keepdims=True))
            weighted = jnp.dot(probabilities.astype(jnp.bfloat16), head_values, preferred_element_type=jnp.float32)
            return weighted / denominator
        outputs.append(lax.map(per_head, (soft_q[:, first_row:key_end], head_ids)))
    return jnp.concatenate(outputs, axis=1)

def reference(lin_q, lin_k, lin_v, log_decay, prior_state, lin_gain, soft_q, span_k, span_v, cache_k, cached_value_rows, cache_len):
    lightning_normalized_result = full_norm(lightning(lin_q, lin_k, lin_v, log_decay, prior_state), lin_gain)
    soft_out = softmax_attention(soft_q, span_k, span_v, cache_k, cached_value_rows, cache_len).astype(jnp.bfloat16)
    return (lightning_normalized_result, soft_out)
```

```python
import functools
import math

import jax
import jax.numpy as jnp
from jax import lax
from jax.experimental import pallas as pl
from jax.experimental.pallas import tpu as pltpu
from jax.sharding import PartitionSpec as P

GROUP_Q = 8
N_Z, N_Y, N_CORE = 4, 4, 2
N_CTX = N_Z * N_Y * N_CORE
N_YC = N_Y * N_CORE
HD = 128
HEADS_DEV = 4
TOK = 256
CROWS = 128
PAY = 2 * TOK + 2 * CROWS
KCHUNK = 1024
MASK_FILL = -1e30
LOG2E = 1.4426950408889634
VMEM_LIMIT = 48 * 1024 * 1024

F32 = jnp.float32
BF16 = jnp.bfloat16

Z_GROUPS = [[z * N_YC + r for z in range(N_Z)] for r in range(N_YC)]
YC_GROUPS = [[z * N_YC + r for r in range(N_YC)] for z in range(N_Z)]

NT = (((1,), (1,)), ((), ()))
NN = (((1,), (0,)), ((), ()))
TN = (((0,), (0,)), ((), ()))


def dot(a, b, dims):
    return lax.dot_general(a, b, dims, preferred_element_type=F32)


def split3(x):
    hi = x.astype(BF16)
    rest = x - hi.astype(F32)
    mid = rest.astype(BF16)
    low = (rest - mid.astype(F32)).astype(BF16)
    return hi, mid, low


def split2(x):
    hi = x.astype(BF16)
    return hi, (x - hi.astype(F32)).astype(BF16)


def pack_kernel(head_ref, sk_ref, sv_ref, ck_ref, cv_ref, out_ref):
    out_ref[0:TOK, :] = sk_ref[0]
    out_ref[TOK : 2 * TOK, :] = sv_ref[0]
    out_ref[2 * TOK : 2 * TOK + CROWS, :] = ck_ref[0]
    out_ref[2 * TOK + CROWS : PAY, :] = cv_ref[0]


def pack(kv_head, span_k, span_v, cache_k, cache_v):
    def spec(rows):
        return pl.BlockSpec((1, rows, HD), lambda i, h: (h[0], 0, 0))

    return pl.pallas_call(
        pack_kernel,
        out_shape=jax.ShapeDtypeStruct((PAY, HD), BF16),
        grid_spec=pltpu.PrefetchScalarGridSpec(
            num_scalar_prefetch=1,
            grid=(1,),
            in_specs=[spec(TOK), spec(TOK), spec(CROWS), spec(CROWS)],
            out_specs=pl.BlockSpec((PAY, HD), lambda i, h: (0, 0)),
        ),
        name="pack_kv",
    )(kv_head, span_k, span_v, cache_k, cache_v)


def lightning_local_kernel(place_ref, q_ref, k_ref, v_ref, decay_ref, prior_ref, mixed_ref, cum_ref, pay_ref):
    first = jnp.where(place_ref[0] == 0, 1.0, 0.0).astype(F32)
    t_ids = lax.broadcasted_iota(jnp.int32, (TOK, TOK), 0)
    s_ids = lax.broadcasted_iota(jnp.int32, (TOK, TOK), 1)
    lower = t_ids >= s_ids
    tri = jnp.where(lower, 1.0, 0.0).astype(BF16)
    parts = split3(jnp.concatenate([decay_ref[...], decay_ref[...]], axis=0))
    cum_rows = sum(dot(p, tri, NT) for p in parts)
    cum_cols = sum(dot(tri, p, NT) for p in parts)
    cum_ref[...] = cum_cols
    pieces = HD // 16
    for h in range(HEADS_DEV):
        row = cum_rows[h : h + 1, :]
        col = cum_cols[:, h : h + 1]
        final = cum_rows[h : h + 1, TOK - 1 : TOK]
        q, k, v = q_ref[h], k_ref[h], v_ref[h]
        gap = jnp.where(lower, col - row, 0.0)
        weights = jnp.where(lower, dot(q, k, NT) * jnp.exp(gap), 0.0).astype(BF16)
        mixed_ref[h] = dot(weights, v, NN)
        keyed_hi, keyed_lo = split2(k.astype(F32) * jnp.exp(final - col))
        state = dot(keyed_hi, v, TN) + dot(keyed_lo, v, TN)
        state = state + (first * jnp.exp(final)) * prior_ref[h]
        pay_ref[h * pieces : (h + 1) * pieces, 0:16, :] = state.astype(BF16).reshape(pieces, 16, HD)
        line = jnp.broadcast_to(final, (16, HD))
        d_hi, d_mid, d_low = (p.astype(F32) for p in split3(line))
        ids = lax.broadcasted_iota(jnp.int32, (16, HD), 0)
        block = jnp.where(ids == 0, d_hi, jnp.where(ids == 1, d_mid, d_low)).astype(BF16)
        for i in range(pieces):
            pay_ref[h * pieces + i, 16:32, :] = block


def lightning_local(place, lin_q, lin_k, lin_v, log_decay, prior_state):
    vmem = pl.BlockSpec(memory_space=pltpu.VMEM)
    return pl.pallas_call(
        lightning_local_kernel,
        out_shape=(
            jax.ShapeDtypeStruct((HEADS_DEV, TOK, HD), F32),
            jax.ShapeDtypeStruct((TOK, 2 * HEADS_DEV), F32),
            jax.ShapeDtypeStruct((N_CTX, 32, HD), BF16),
        ),
        in_specs=[pl.BlockSpec(memory_space=pltpu.SMEM)] + [vmem] * 5,
        out_specs=(vmem, vmem, vmem),
        compiler_params=pltpu.CompilerParams(vmem_limit_bytes=VMEM_LIMIT),
        name="lightning_local",
    )(place, lin_q, lin_k, lin_v, log_decay, prior_state)


def scan_kernel(in_ref, out_ref):
    acc = jnp.zeros((16, HD), F32)
    for c in range(N_CTX):
        out_ref[c] = acc.astype(BF16)
        if c + 1 < N_CTX:
            tail = in_ref[c, 16:32, :].astype(F32)
            decay = tail[0:1] + tail[1:2] + tail[2:3]
            acc = acc * jnp.exp(decay) + in_ref[c, 0:16, :].astype(F32)


def scan_pieces(pieces):
    vmem = pl.BlockSpec(memory_space=pltpu.VMEM)
    return pl.pallas_call(
        scan_kernel,
        out_shape=jax.ShapeDtypeStruct((N_CTX, 16, HD), BF16),
        in_specs=[vmem],
        out_specs=vmem,
        name="scan_states",
    )(pieces)


def lightning_mix_kernel(place_ref, q_ref, mixed_ref, cum_ref, carried_ref, prior_ref, out_ref, square_ref):
    first = place_ref[0] == 0
    total = jnp.zeros((TOK, HD), F32)
    for h in range(HEADS_DEV):
        state = jnp.where(first, prior_ref[h], carried_ref[h].astype(F32))
        hi, low = split2(state)
        q = q_ref[h]
        inter = dot(q, hi, NN) + dot(q, low, NN)
        mixed = mixed_ref[h] + jnp.exp(cum_ref[:, h : h + 1]) * inter
        out_ref[h] = mixed
        total = total + mixed * mixed
    ones = jnp.ones((8, HD), BF16)
    square_ref[...] = sum(dot(ones, p, NT) for p in split3(total))


def lightning_mix(place, lin_q, mixed, cum, carried, prior_state):
    vmem = pl.BlockSpec(memory_space=pltpu.VMEM)
    return pl.pallas_call(
        lightning_mix_kernel,
        out_shape=(
            jax.ShapeDtypeStruct((HEADS_DEV, TOK, HD), F32),
            jax.ShapeDtypeStruct((8, TOK), F32),
        ),
        in_specs=[pl.BlockSpec(memory_space=pltpu.SMEM)] + [vmem] * 5,
        out_specs=(vmem, vmem),
        compiler_params=pltpu.CompilerParams(vmem_limit_bytes=VMEM_LIMIT),
        name="lightning_mix",
    )(place, lin_q, mixed, cum, carried, prior_state)


def norm_kernel(count, mixed_ref, squares_ref, gain_ref, out_ref):
    total = jnp.sum(squares_ref[...], axis=0)
    inv = lax.rsqrt(total * (1.0 / count) + 1e-05)
    t_ids = lax.broadcasted_iota(jnp.int32, (HD, HD), 0)
    s_ids = lax.broadcasted_iota(jnp.int32, (HD, HD), 1)
    for half in range(TOK // HD):
        diag = jnp.where(t_ids == s_ids, jnp.broadcast_to(inv[half : half + 1, :], (HD, HD)), 0.0)
        col = jnp.sum(diag, axis=1, keepdims=True)
        rows = slice(half * HD, (half + 1) * HD)
        for h in range(HEADS_DEV):
            out_ref[h, rows, :] = (mixed_ref[h, rows, :] * col * gain_ref[h : h + 1, :]).astype(BF16)


def lightning_norm(count, mixed, squares, gain):
    vmem = pl.BlockSpec(memory_space=pltpu.VMEM)
    return pl.pallas_call(
        functools.partial(norm_kernel, float(count)),
        out_shape=jax.ShapeDtypeStruct((HEADS_DEV, TOK, HD), BF16),
        in_specs=[vmem] * 3,
        out_specs=vmem,
        compiler_params=pltpu.CompilerParams(vmem_limit_bytes=VMEM_LIMIT),
        name="lightning_norm",
    )(mixed, squares, gain)


def attention_kernel(scale, info_ref, q_ref, kv_hbm, out_ref, ckv, skv, qs, m_ref, l_ref, acc_ref, csem, ssem):
    place = info_ref[N_CTX]
    last_chunk = place // 4
    n_cache = N_CTX * CROWS // KCHUNK
    yc_step = N_YC // n_cache

    def cache_copy(i):
        return pltpu.make_async_copy(
            kv_hbm.at[pl.ds(i * yc_step, yc_step), :, pl.ds(2 * TOK, 2 * CROWS), :], ckv.at[i], csem.at[i]
        )

    def span_copy(j):
        return pltpu.make_async_copy(
            kv_hbm.at[pl.ds((j % 2) * 4, 4), j // 2, pl.ds(0, 2 * TOK), :], skv.at[j], ssem.at[j]
        )

    for i in range(n_cache):
        cache_copy(i).start()

    def start(j, _):
        span_copy(j).start()
        return 0

    lax.fori_loop(0, last_chunk + 1, start, 0)

    for h in range(HEADS_DEV):
        hi, low = split2(q_ref[h].astype(F32) * scale)
        qs[h, :, 0:HD] = hi
        qs[h, :, HD : 2 * HD] = low
    m_ref[...] = jnp.full_like(m_ref, MASK_FILL)
    l_ref[...] = jnp.zeros_like(l_ref)
    acc_ref[...] = jnp.zeros_like(acc_ref)

    def update(keys, values, mask):
        wide = jnp.concatenate([keys, keys], axis=1)
        for h in range(HEADS_DEV):
            scores = mask(dot(qs[h], wide, NT))
            m_old = m_ref[h]
            m_new = jnp.maximum(m_old, jnp.max(scores, axis=1, keepdims=True))
            probs = jnp.exp2(scores - m_new[:, 0:1])
            alpha = jnp.exp2(m_old - m_new)
            m_ref[h] = m_new
            l_ref[h] = l_ref[h] * alpha + jnp.sum(probs, axis=1, keepdims=True)
            acc_ref[h] = acc_ref[h] * alpha + dot(probs.astype(BF16), values, NN)

    lanes = lax.broadcasted_iota(jnp.int32, (1, CROWS), 1)

    for i in range(n_cache):
        cache_copy(i).wait()
        bias = []
        for r in range(yc_step):
            for z in range(N_Z):
                live = info_ref[z * N_YC + i * yc_step + r]
                bias.append(jnp.where(lanes < live, 0.0, MASK_FILL).astype(F32))
        bias = jnp.concatenate(bias, axis=1)
        block = ckv[i].reshape(yc_step * N_Z, 2, CROWS, HD)
        update(
            block[:, 0].reshape(KCHUNK, HD), block[:, 1].reshape(KCHUNK, HD), lambda s: s + bias
        )

    def span_kv(j):
        span_copy(j).wait()
        block = skv[j].reshape(4, 2, TOK, HD)
        return block[:, 0].reshape(KCHUNK, HD), block[:, 1].reshape(KCHUNK, HD)

    def full(j, _):
        keys, values = span_kv(j)
        update(keys, values, lambda s: s)
        return 0

    lax.fori_loop(0, last_chunk, full, 0)
    keys, values = span_kv(last_chunk)
    offset = (place - last_chunk * 4) * TOK
    rows = lax.broadcasted_iota(jnp.int32, (TOK, KCHUNK), 0) + offset
    cols = lax.broadcasted_iota(jnp.int32, (TOK, KCHUNK), 1)
    update(keys, values, lambda s: jnp.where(cols <= rows, s, MASK_FILL))
    for h in range(HEADS_DEV):
        out_ref[h] = (acc_ref[h] / l_ref[h]).astype(BF16)


def attention(info, soft_q, kv):
    vmem = pl.BlockSpec(memory_space=pltpu.VMEM)
    n_cache = N_CTX * CROWS // KCHUNK
    n_span = N_CTX * TOK // KCHUNK
    stat = pltpu.VMEM((HEADS_DEV, TOK, HD), F32)
    return pl.pallas_call(
        functools.partial(attention_kernel, LOG2E / math.sqrt(HD)),
        out_shape=jax.ShapeDtypeStruct((HEADS_DEV, TOK, HD), BF16),
        in_specs=[pl.BlockSpec(memory_space=pltpu.SMEM), vmem, pl.BlockSpec(memory_space=pl.ANY)],
        out_specs=vmem,
        scratch_shapes=[
            pltpu.VMEM((n_cache, N_YC // n_cache, N_Z, 2 * CROWS, HD), BF16),
            pltpu.VMEM((n_span, 4, 2 * TOK, HD), BF16),
            pltpu.VMEM((HEADS_DEV, TOK, 2 * HD), BF16),
            stat,
            stat,
            stat,
            pltpu.SemaphoreType.DMA((n_cache,)),
            pltpu.SemaphoreType.DMA((n_span,)),
        ],
        compiler_params=pltpu.CompilerParams(vmem_limit_bytes=VMEM_LIMIT),
        name="softmax_attention",
    )(info, soft_q, kv)


def per_device(
    lin_q,
    lin_k,
    lin_v,
    log_decay,
    prior_state,
    lin_gain,
    soft_q,
    span_k,
    span_v,
    cache_k,
    cached_value_rows,
    cache_len,
):
    ctx = lax.axis_index("ctx").astype(jnp.int32)
    tp = lax.axis_index("tp").astype(jnp.int32)
    place = ctx.reshape(1)
    kv_head = (tp * HEADS_DEV // GROUP_Q).reshape(1)

    payload = pack(kv_head, span_k, span_v, cache_k, cached_value_rows)
    column = lax.all_gather(payload, "ctx", axis=0, tiled=True, axis_index_groups=Z_GROUPS)
    kv = lax.all_gather(column, "ctx", axis=0, tiled=True, axis_index_groups=YC_GROUPS)
    kv = kv.reshape(N_YC, N_Z, PAY, HD)

    mixed, cum, pay = lightning_local(place, lin_q, lin_k, lin_v, log_decay, prior_state)
    pieces = lax.all_to_all(pay, "ctx", 0, 0)
    prefixes = scan_pieces(pieces)
    carried = lax.all_to_all(prefixes, "ctx", 0, 0).reshape(HEADS_DEV, HD, HD)
    mixed, squares = lightning_mix(place, lin_q, mixed, cum, carried, prior_state)
    n_tp = lax.axis_size("tp")
    own = squares[0].reshape(1, TOK // HD, HD)
    all_squares = lax.all_to_all(jnp.broadcast_to(own, (n_tp, TOK // HD, HD)), "tp", 0, 0)
    normalized = lightning_norm(n_tp * HEADS_DEV * HD, mixed, all_squares, lin_gain)

    info = jnp.concatenate([cache_len, place])
    soft_out = attention(info, soft_q, kv)
    return (normalized, soft_out)


def solution(mesh):
    placed = (
        P("tp", "ctx", None),
        P("tp", "ctx", None),
        P("tp", "ctx", None),
        P("tp", "ctx"),
        P("tp", None, None),
        P("tp", None),
        P("tp", "ctx", None),
        P(None, "ctx", None),
        P(None, "ctx", None),
        P(None, "ctx", None),
        P(None, "ctx", None),
        P(),
    )
    return jax.shard_map(
        per_device,
        mesh=mesh,
        in_specs=placed,
        out_specs=(P("tp", "ctx", None), P("tp", "ctx", None)),
        check_vma=False,
    )
```

```python
import functools
import math

import jax
import jax.numpy as jnp
from jax import lax
from jax.experimental import pallas as pl
from jax.experimental.pallas import tpu as pltpu
from jax.sharding import PartitionSpec as P

GROUP_Q = 8
N_Z, N_Y, N_CORE = 4, 4, 2
N_CTX = N_Z * N_Y * N_CORE
N_YC = N_Y * N_CORE
HD = 128
HEADS_DEV = 4
TOK = 256
CROWS = 128
KROWS = TOK + CROWS
PAY = 2 * KROWS
D_ROWS = 16
S_ROWS = HEADS_DEV * HD + D_ROWS
HEADS_CORE = HEADS_DEV // N_CORE
U_ROWS = HEADS_CORE * HD + D_ROWS
MASK_FILL = -1e30
LOG2E = 1.4426950408889634
VMEM_LIMIT = 60 * 1024 * 1024

F32 = jnp.float32
BF16 = jnp.bfloat16

Z_GROUPS = [[z * N_YC + r for z in range(N_Z)] for r in range(N_YC)]
YC_GROUPS = [[z * N_YC + r for r in range(N_YC)] for z in range(N_Z)]
CORE_GROUPS = [[N_CORE * r + i for i in range(N_CORE)] for r in range(N_CTX // N_CORE)]

NT = (((1,), (1,)), ((), ()))
NN = (((1,), (0,)), ((), ()))
TN = (((0,), (0,)), ((), ()))


def dot(a, b, dims):
    return lax.dot_general(a, b, dims, preferred_element_type=F32)


def split3(x):
    hi = x.astype(BF16)
    rest = x - hi.astype(F32)
    mid = rest.astype(BF16)
    low = (rest - mid.astype(F32)).astype(BF16)
    return hi, mid, low


def split2(x):
    hi = x.astype(BF16)
    return hi, (x - hi.astype(F32)).astype(BF16)


HBM = pl.BlockSpec(memory_space=pltpu.HBM)
VMEM = pl.BlockSpec(memory_space=pltpu.VMEM)
SMEM = pl.BlockSpec(memory_space=pltpu.SMEM)
LIN = (HEADS_DEV, TOK, HD)
STATE = (HEADS_DEV, HD, HD)


def begin(pairs, sems, base=0):
    copies = [pltpu.make_async_copy(a, b, sems.at[base + i]) for i, (a, b) in enumerate(pairs)]
    for copy in copies:
        copy.start()
    return copies


def finish(copies):
    for copy in copies:
        copy.wait()


def run(kernel, name, operands, in_specs, outs, scratch, n_sems):
    single = len(outs) == 1
    shapes = tuple(jax.ShapeDtypeStruct(shape, kind) for shape, kind, _ in outs)
    specs = tuple(spec for _, _, spec in outs)
    return pl.pallas_call(
        kernel,
        out_shape=shapes[0] if single else shapes,
        in_specs=in_specs,
        out_specs=specs[0] if single else specs,
        scratch_shapes=[pltpu.VMEM(shape, kind) for shape, kind in scratch]
        + [pltpu.SemaphoreType.DMA((n_sems,))],
        compiler_params=pltpu.CompilerParams(vmem_limit_bytes=VMEM_LIMIT),
        name=name,
    )(*operands)


def decay_lines(values):
    ids = lax.broadcasted_iota(jnp.int32, (D_ROWS, HD), 0)
    lines = jnp.zeros((D_ROWS, HD), F32)
    for h, value in enumerate(values):
        for i, part in enumerate(split3(jnp.broadcast_to(value, (1, HD)))):
            lines = jnp.where(ids == 3 * h + i, part.astype(F32), lines)
    return lines.astype(BF16)


def decay_of(lines, h):
    lines = lines[3 * h : 3 * h + 3].astype(F32)
    return lines[0:1] + lines[1:2] + lines[2:3]


def prep_kernel(
    info_ref, sk_hbm, sv_hbm, ck_hbm, cv_hbm, q_hbm, k_hbm, v_hbm, decay_hbm, prior_hbm,
    payload_hbm, plane_hbm, mixed_hbm, cum_hbm,
    kv_ref, q_ref, k_ref, v_ref, decay_ref, prior_ref, mixed_ref, cum_ref, state_ref, sems,
):
    head = info_ref[0]
    packs = begin(
        [
            (sk_hbm.at[head], kv_ref.at[pl.ds(0, TOK), :]),
            (ck_hbm.at[head], kv_ref.at[pl.ds(TOK, CROWS), :]),
            (sv_hbm.at[head], kv_ref.at[pl.ds(KROWS, TOK), :]),
            (cv_hbm.at[head], kv_ref.at[pl.ds(KROWS + TOK, CROWS), :]),
        ],
        sems,
    )
    loads = begin(
        [(decay_hbm, decay_ref), (q_hbm, q_ref), (k_hbm, k_ref), (v_hbm, v_ref), (prior_hbm, prior_ref)],
        sems,
        4,
    )
    finish(packs)
    packs = begin([(kv_ref, payload_hbm), (kv_ref, plane_hbm.at[pl.ds(0, PAY), :])], sems, 9)
    finish(loads)
    first = jnp.where(info_ref[1] == 0, 1.0, 0.0).astype(F32)
    t_ids = lax.broadcasted_iota(jnp.int32, (TOK, TOK), 0)
    s_ids = lax.broadcasted_iota(jnp.int32, (TOK, TOK), 1)
    lower = t_ids >= s_ids
    tri = jnp.where(lower, 1.0, 0.0).astype(BF16)
    parts = split3(jnp.concatenate([decay_ref[...], decay_ref[...]], axis=0))
    cum_rows = sum(dot(p, tri, NT) for p in parts)
    cum_cols = sum(dot(tri, p, NT) for p in parts)
    cum_ref[...] = cum_cols
    finals = []
    for h in range(HEADS_DEV):
        row = cum_rows[h : h + 1, :]
        col = cum_cols[:, h : h + 1]
        final = cum_rows[h : h + 1, TOK - 1 : TOK]
        finals.append(final)
        q, k, v = q_ref[h], k_ref[h], v_ref[h]
        gap = jnp.where(lower, col - row, 0.0)
        weights = jnp.where(lower, dot(q, k, NT) * jnp.exp(gap), 0.0).astype(BF16)
        mixed_ref[h] = dot(weights, v, NN)
        keyed_hi, keyed_lo = split2(k.astype(F32) * jnp.exp(final - col))
        state = dot(keyed_hi, v, TN) + dot(keyed_lo, v, TN)
        state = state + (first * jnp.exp(final)) * prior_ref[h]
        state_ref[h * HD : (h + 1) * HD, :] = state.astype(BF16)
    state_ref[HEADS_DEV * HD : S_ROWS, :] = decay_lines(finals)
    stores = begin(
        [
            (state_ref, plane_hbm.at[pl.ds(PAY, S_ROWS), :]),
            (mixed_ref, mixed_hbm),
            (cum_ref, cum_hbm),
        ],
        sems,
        11,
    )
    finish(packs)
    finish(stores)


def prep(info, *arrays):
    cum = (TOK, 2 * HEADS_DEV)
    return run(
        prep_kernel,
        "prep",
        (info, *arrays),
        [SMEM] + [HBM] * len(arrays),
        [((PAY, HD), BF16, HBM), ((PAY + S_ROWS, HD), BF16, HBM), (LIN, F32, HBM), (cum, F32, HBM)],
        [
            ((PAY, HD), BF16),
            (LIN, BF16), (LIN, BF16), (LIN, BF16), ((HEADS_DEV, TOK), F32), (STATE, F32),
            (LIN, F32), (cum, F32), ((S_ROWS, HD), BF16),
        ],
        14,
    )


def roll_kernel(info_ref, in_hbm, out_hbm, kv_ref, sems):
    z = info_ref[1] // N_YC
    loads = begin([(in_hbm.at[(z + 1 + i) % N_Z], kv_ref.at[i]) for i in range(N_Z - 1)], sems)
    stores = []
    for i, load in enumerate(loads):
        load.wait()
        stores += begin([(kv_ref.at[i], out_hbm.at[i])], sems, N_Z - 1 + i)
    finish(stores)


def other_planes(info, column):
    shape = (N_Z - 1, PAY, HD)
    return run(
        roll_kernel,
        "other_planes",
        (info, column),
        [SMEM, HBM],
        [(shape, BF16, HBM)],
        [(shape, BF16)],
        2 * (N_Z - 1),
    )


def plane_scan_kernel(info_ref, plane_hbm, own_hbm, own_decay_ref, total_hbm, states, own_ref, total_ref, sems):
    finish(begin([(plane_hbm.at[:, pl.ds(PAY, S_ROWS), :], states)], sems))
    place = info_ref[1] % N_YC
    finals = []
    for h in range(HEADS_DEV):
        rows = slice(h * HD, (h + 1) * HD)
        acc = jnp.zeros((HD, HD), F32)
        run = jnp.zeros((1, HD), F32)
        own, own_run = acc, run
        for r in range(N_YC):
            own = jnp.where(place == r, acc, own)
            own_run = jnp.where(place == r, run, own_run)
            decay = decay_of(states[r, HEADS_DEV * HD : S_ROWS, :], h)
            acc = acc * jnp.exp(decay) + states[r, rows, :].astype(F32)
            run = run + decay
        own_ref[h] = own
        own_decay_ref[h : h + 1, :] = own_run
        total_ref[rows, :] = acc.astype(BF16)
        finals.append(run)
    total_ref[HEADS_DEV * HD : S_ROWS, :] = decay_lines(finals)
    first = (info_ref[1] % N_CORE) * (HEADS_CORE * HD)
    pairs = [(own_ref, own_hbm)]
    for z in range(N_Z):
        pairs.append((total_ref.at[pl.ds(first, HEADS_CORE * HD), :], total_hbm.at[z, pl.ds(0, HEADS_CORE * HD), :]))
        pairs.append(
            (total_ref.at[pl.ds(HEADS_DEV * HD, D_ROWS), :], total_hbm.at[z, pl.ds(HEADS_CORE * HD, D_ROWS), :])
        )
    finish(begin(pairs, sems, 1))


def plane_scan(info, plane):
    return run(
        plane_scan_kernel,
        "plane_scan",
        (info, plane),
        [SMEM, HBM],
        [(STATE, F32, HBM), ((HEADS_DEV, HD), F32, VMEM), ((N_Z, U_ROWS, HD), BF16, HBM)],
        [((N_YC, S_ROWS, HD), BF16), (STATE, F32), ((S_ROWS, HD), BF16)],
        2 + 2 * N_Z,
    )


def lightning_mix_kernel(
    info_ref, q_hbm, mixed_hbm, cum_hbm, own_hbm, own_decay_ref, totals_hbm, prior_hbm,
    out_hbm, square_ref,
    q_ref, mixed_ref, cum_ref, own_ref, totals_ref, prior_ref, out_ref, sems,
):
    loads = begin(
        [
            (totals_hbm, totals_ref), (own_hbm, own_ref), (prior_hbm, prior_ref),
            (cum_hbm, cum_ref), (q_hbm, q_ref), (mixed_hbm, mixed_ref),
        ],
        sems,
    )
    finish(loads)
    place = info_ref[1]
    z_place = place // N_YC
    total = jnp.zeros((TOK, HD), F32)
    for h in range(HEADS_DEV):
        core, inner = h // HEADS_CORE, h % HEADS_CORE
        rows = slice(inner * HD, (inner + 1) * HD)
        acc = jnp.zeros((HD, HD), F32)
        for z in range(N_Z - 1):
            decay = decay_of(totals_ref[core, z, HEADS_CORE * HD : U_ROWS, :], h)
            nxt = acc * jnp.exp(decay) + totals_ref[core, z, rows, :].astype(F32)
            acc = jnp.where(z < z_place, nxt, acc)
        state = own_ref[h] + jnp.exp(own_decay_ref[h : h + 1, :]) * acc
        state = jnp.where(place == 0, prior_ref[h], state)
        hi, low = split2(state)
        q = q_ref[h]
        inter = dot(q, hi, NN) + dot(q, low, NN)
        mixed = mixed_ref[h] + jnp.exp(cum_ref[:, h : h + 1]) * inter
        out_ref[h] = mixed
        total = total + mixed * mixed
    ones = jnp.ones((8, HD), BF16)
    stores = begin([(out_ref, out_hbm)], sems, 6)
    squares = sum(dot(ones, p, NT) for p in split3(total))
    for half in range(TOK // HD):
        line = squares[0:1, half * HD : (half + 1) * HD]
        square_ref[:, half, :] = jnp.broadcast_to(line, (square_ref.shape[0], HD))
    finish(stores)


def lightning_mix(n_tp, info, *arrays):
    specs = [HBM] * len(arrays)
    specs[4] = VMEM
    return run(
        lightning_mix_kernel,
        "lightning_mix",
        (info, *arrays),
        [SMEM] + specs,
        [(LIN, F32, HBM), ((n_tp, TOK // HD, HD), F32, VMEM)],
        [
            (LIN, BF16), (LIN, F32), ((TOK, 2 * HEADS_DEV), F32), (STATE, F32),
            ((N_CORE, N_Z, U_ROWS, HD), BF16), (STATE, F32), (LIN, F32),
        ],
        7,
    )


def norm_kernel(count, mixed_hbm, squares_ref, gain_hbm, out_hbm, mixed_ref, gain_ref, out_ref, sems):
    finish(begin([(mixed_hbm, mixed_ref), (gain_hbm, gain_ref)], sems))
    total = jnp.sum(squares_ref[...], axis=0)
    inv = lax.rsqrt(total * (1.0 / count) + 1e-05)
    t_ids = lax.broadcasted_iota(jnp.int32, (HD, HD), 0)
    s_ids = lax.broadcasted_iota(jnp.int32, (HD, HD), 1)
    for half in range(TOK // HD):
        diag = jnp.where(t_ids == s_ids, jnp.broadcast_to(inv[half : half + 1, :], (HD, HD)), 0.0)
        col = jnp.sum(diag, axis=1, keepdims=True)
        rows = slice(half * HD, (half + 1) * HD)
        for h in range(HEADS_DEV):
            out_ref[h, rows, :] = (mixed_ref[h, rows, :] * col * gain_ref[h : h + 1, :]).astype(BF16)
    finish(begin([(out_ref, out_hbm)], sems, 2))


def lightning_norm(count, mixed, squares, gain):
    return run(
        functools.partial(norm_kernel, float(count)),
        "lightning_norm",
        (mixed, squares, gain),
        [HBM, VMEM, HBM],
        [(LIN, BF16, HBM)],
        [(LIN, F32), ((HEADS_DEV, HD), F32), (LIN, BF16)],
        3,
    )


def cache_bias(info_ref, z, r):
    lanes = lax.broadcasted_iota(jnp.int32, (1, CROWS), 1)
    return jnp.where(lanes < info_ref[2 + z * N_YC + r], 0.0, MASK_FILL).astype(F32)


def with_ones(values):
    return jnp.concatenate([values, jnp.ones(values.shape, BF16)], axis=1)


def wide(stat, width):
    return jnp.concatenate([stat] * (width // HD), axis=1)


def near_kernel(scale, info_ref, q_hbm, plane_hbm, m_hbm, acc_hbm, q_ref, kv, m_ref, acc_ref, sems):
    loads = begin([(q_hbm, q_ref), (plane_hbm.at[:, pl.ds(0, PAY), :], kv)], sems)
    z = info_ref[1] // N_YC
    place = info_ref[1] % N_YC
    rows = lax.broadcasted_iota(jnp.int32, (TOK, TOK), 0)
    cols = lax.broadcasted_iota(jnp.int32, (TOK, TOK), 1)
    ahead = cols - rows
    bias = [cache_bias(info_ref, z, r) for r in range(N_YC)]
    finish(loads)
    stores = []
    keys = kv[:, 0:KROWS, :].reshape(N_YC * KROWS, HD)
    values = with_ones(kv[:, KROWS:PAY, :].reshape(N_YC * KROWS, HD))
    for h in range(HEADS_DEV):
        raw = dot(q_ref[h], keys, NT)
        pieces = []
        for r in range(N_YC):
            span = raw[:, r * KROWS : r * KROWS + TOK]
            pieces.append(jnp.where(ahead <= (place - r) * TOK, span, MASK_FILL))
            pieces.append(raw[:, r * KROWS + TOK : (r + 1) * KROWS] + bias[r])
        raw = jnp.concatenate(pieces, axis=1)
        peak = jnp.broadcast_to(jnp.max(raw, axis=1, keepdims=True), (TOK, HD))
        probs = jnp.exp2((raw - wide(peak, N_YC * KROWS)) * scale)
        m_ref[h] = peak
        acc_ref[h] = dot(probs.astype(BF16), values, NN)
        stores += begin([(m_ref.at[h], m_hbm.at[h]), (acc_ref.at[h], acc_hbm.at[h])], sems, 2 + 2 * h)
    finish(stores)


SUMS = (HEADS_DEV, TOK, 2 * HD)


def near_attention(info, soft_q, plane):
    return run(
        functools.partial(near_kernel, LOG2E / math.sqrt(HD)),
        "near_attention",
        (info, soft_q, plane),
        [SMEM, HBM, HBM],
        [(LIN, F32, HBM), (SUMS, F32, HBM)],
        [(LIN, BF16), ((N_YC, PAY, HD), BF16), (LIN, F32), (SUMS, F32)],
        2 + 2 * HEADS_DEV,
    )


def far_kernel(
    scale, info_ref, q_hbm, m_hbm, acc_hbm, kv_hbm, out_hbm, q_ref, m_ref, acc_ref, kv, out_ref, sems
):
    loads = begin([(q_hbm, q_ref), (m_hbm, m_ref), (acc_hbm, acc_ref)], sems, N_Z - 1)
    begin([(kv_hbm.at[:, i, :, :], kv.at[i]) for i in range(N_Z - 1)], sems)
    finish(loads)
    z_place = info_ref[1] // N_YC

    def update(h, raw, values):
        m_old = m_ref[h]
        m_new = jnp.maximum(m_old, jnp.max(raw, axis=1, keepdims=True))
        probs = jnp.exp2((raw - wide(m_new, raw.shape[1])) * scale)
        alpha = jnp.exp2((m_old - m_new) * scale)
        m_ref[h] = m_new
        acc_ref[h] = acc_ref[h] * wide(alpha, 2 * HD) + dot(probs.astype(BF16), values, NN)

    def fold(i, _):
        pltpu.make_async_copy(kv_hbm.at[:, i, :, :], kv.at[i], sems.at[i]).wait()
        z = (z_place + 1 + i) % N_Z
        bias = [cache_bias(info_ref, z, r) for r in range(N_YC)]

        @pl.when(z < z_place)
        def whole():
            keys = kv[i, :, 0:KROWS, :].reshape(N_YC * KROWS, HD)
            values = with_ones(kv[i, :, KROWS:PAY, :].reshape(N_YC * KROWS, HD))
            for h in range(HEADS_DEV):
                raw = dot(q_ref[h], keys, NT)
                pieces = []
                for r in range(N_YC):
                    pieces.append(raw[:, r * KROWS : r * KROWS + TOK])
                    pieces.append(raw[:, r * KROWS + TOK : (r + 1) * KROWS] + bias[r])
                update(h, jnp.concatenate(pieces, axis=1), values)

        @pl.when(z > z_place)
        def cache_only():
            keys = kv[i, :, TOK:KROWS, :].reshape(N_YC * CROWS, HD)
            values = with_ones(kv[i, :, KROWS + TOK : PAY, :].reshape(N_YC * CROWS, HD))
            line = jnp.concatenate(bias, axis=1)
            for h in range(HEADS_DEV):
                update(h, dot(q_ref[h], keys, NT) + line, values)

        return 0

    lax.fori_loop(0, N_Z - 1, fold, 0)
    stores = []
    for h in range(HEADS_DEV):
        acc = acc_ref[h]
        out_ref[h] = (acc[:, 0:HD] / acc[:, HD : 2 * HD]).astype(BF16)
        stores += begin([(out_ref.at[h], out_hbm.at[h])], sems, N_Z + 2 + h)
    finish(stores)


def far_attention(info, soft_q, peaks, sums, kv):
    return run(
        functools.partial(far_kernel, LOG2E / math.sqrt(HD)),
        "far_attention",
        (info, soft_q, peaks, sums, kv),
        [SMEM] + [HBM] * 4,
        [(LIN, BF16, HBM)],
        [(LIN, BF16), (LIN, F32), (SUMS, F32), ((N_Z - 1, N_YC, PAY, HD), BF16), (LIN, BF16)],
        N_Z + 2 + HEADS_DEV,
    )


def per_device(
    lin_q,
    lin_k,
    lin_v,
    log_decay,
    prior_state,
    lin_gain,
    soft_q,
    span_k,
    span_v,
    cache_k,
    cached_value_rows,
    cache_len,
):
    ctx = lax.axis_index("ctx").astype(jnp.int32)
    tp = lax.axis_index("tp").astype(jnp.int32)
    kv_head = tp * HEADS_DEV // GROUP_Q
    info = jnp.concatenate([kv_head.reshape(1), ctx.reshape(1), cache_len])

    payload, plane_payload, mixed, cum = prep(
        info, span_k, span_v, cache_k, cached_value_rows, lin_q, lin_k, lin_v, log_decay, prior_state
    )
    plane = lax.all_gather(plane_payload, "ctx", axis=0, tiled=True, axis_index_groups=YC_GROUPS)
    plane = plane.reshape(N_YC, PAY + S_ROWS, HD)
    column = lax.all_gather(payload, "ctx", axis=0, tiled=True, axis_index_groups=Z_GROUPS)
    rest = other_planes(info, column.reshape(N_Z, PAY, HD))
    far = lax.all_gather(
        rest.reshape((N_Z - 1) * PAY, HD), "ctx", axis=0, tiled=True, axis_index_groups=YC_GROUPS
    )
    far = far.reshape(N_YC, N_Z - 1, PAY, HD)

    own, own_decay, plane_totals = plane_scan(info, plane)
    totals = lax.all_to_all(plane_totals, "ctx", 0, 0, axis_index_groups=Z_GROUPS)
    totals = lax.all_gather(totals, "ctx", axis=0, axis_index_groups=CORE_GROUPS)
    peaks, sums = near_attention(info, soft_q, plane)
    own, peaks = lax.optimization_barrier((own, peaks))
    n_tp = lax.axis_size("tp")
    mixed, squares = lightning_mix(n_tp, info, lin_q, mixed, cum, own, own_decay, totals, prior_state)
    squares, peaks = lax.optimization_barrier((squares, peaks))
    all_squares = lax.all_to_all(squares, "tp", 0, 0)
    soft_out = far_attention(info, soft_q, peaks, sums, far)
    mixed, soft_out = lax.optimization_barrier((mixed, soft_out))
    normalized = lightning_norm(n_tp * HEADS_DEV * HD, mixed, all_squares, lin_gain)
    return (normalized, soft_out)


def solution(mesh):
    placed = (
        P("tp", "ctx", None),
        P("tp", "ctx", None),
        P("tp", "ctx", None),
        P("tp", "ctx"),
        P("tp", None, None),
        P("tp", None),
        P("tp", "ctx", None),
        P(None, "ctx", None),
        P(None, "ctx", None),
        P(None, "ctx", None),
        P(None, "ctx", None),
        P(),
    )
    return jax.shard_map(
        per_device,
        mesh=mesh,
        in_specs=placed,
        out_specs=(P("tp", "ctx", None), P("tp", "ctx", None)),
        check_vma=False,
    )
```

```python
import functools
import math

import jax
import jax.numpy as jnp
from jax import lax
from jax.experimental import pallas as pl
from jax.experimental.pallas import tpu as pltpu
from jax.sharding import PartitionSpec as P

GROUP_Q = 8
N_Z, N_Y, N_CORE = 4, 4, 2
N_CTX = N_Z * N_Y * N_CORE
N_YC = N_Y * N_CORE
N_FAR = N_YC - 1
HD = 128
HEADS_DEV = 4
TOK = 256
CROWS = 128
KROWS = TOK + CROWS
PAY = 2 * KROWS
D_ROWS = 16
S_ROWS = HEADS_DEV * HD + D_ROWS
HEADS_CORE = HEADS_DEV // N_CORE
U_ROWS = HEADS_CORE * HD + D_ROWS
MASK_FILL = -1e30
LOG2E = 1.4426950408889634
VMEM_LIMIT = 60 * 1024 * 1024

F32 = jnp.float32
BF16 = jnp.bfloat16

Z_GROUPS = [[z * N_YC + r for z in range(N_Z)] for r in range(N_YC)]
YC_GROUPS = [[z * N_YC + r for r in range(N_YC)] for z in range(N_Z)]
CORE_GROUPS = [[N_CORE * r + i for i in range(N_CORE)] for r in range(N_CTX // N_CORE)]

NT = (((1,), (1,)), ((), ()))
NN = (((1,), (0,)), ((), ()))
TN = (((0,), (0,)), ((), ()))


def dot(a, b, dims):
    return lax.dot_general(a, b, dims, preferred_element_type=F32)


def split3(x):
    hi = x.astype(BF16)
    rest = x - hi.astype(F32)
    mid = rest.astype(BF16)
    low = (rest - mid.astype(F32)).astype(BF16)
    return hi, mid, low


def split2(x):
    hi = x.astype(BF16)
    return hi, (x - hi.astype(F32)).astype(BF16)


HBM = pl.BlockSpec(memory_space=pltpu.HBM)
VMEM = pl.BlockSpec(memory_space=pltpu.VMEM)
SMEM = pl.BlockSpec(memory_space=pltpu.SMEM)
LIN = (HEADS_DEV, TOK, HD)
STATE = (HEADS_DEV, HD, HD)
CUM = (TOK, 2 * HEADS_DEV)


def ctx_place():
    return lax.axis_index("ctx").astype(jnp.int32)


def begin(pairs, sems, base=0):
    copies = [pltpu.make_async_copy(a, b, sems.at[base + i]) for i, (a, b) in enumerate(pairs)]
    for copy in copies:
        copy.start()
    return copies


def finish(copies):
    for copy in copies:
        copy.wait()


def run(kernel, name, operands, in_specs, outs, scratch, n_sems):
    single = len(outs) == 1
    shapes = tuple(jax.ShapeDtypeStruct(shape, kind) for shape, kind, _ in outs)
    specs = tuple(spec for _, _, spec in outs)
    return pl.pallas_call(
        kernel,
        out_shape=shapes[0] if single else shapes,
        in_specs=in_specs,
        out_specs=specs[0] if single else specs,
        scratch_shapes=[pltpu.VMEM(shape, kind) for shape, kind in scratch]
        + [pltpu.SemaphoreType.DMA((n_sems,))],
        compiler_params=pltpu.CompilerParams(vmem_limit_bytes=VMEM_LIMIT),
        name=name,
    )(*operands)


def decay_lines(values):
    ids = lax.broadcasted_iota(jnp.int32, (D_ROWS, HD), 0)
    lines = jnp.zeros((D_ROWS, HD), F32)
    for h, value in enumerate(values):
        for i, part in enumerate(split3(jnp.broadcast_to(value, (1, HD)))):
            lines = jnp.where(ids == 3 * h + i, part.astype(F32), lines)
    return lines.astype(BF16)


def decay_of(lines, h):
    lines = lines[3 * h : 3 * h + 3].astype(F32)
    return lines[0:1] + lines[1:2] + lines[2:3]


def decay_sums(decay_ref):
    t_ids = lax.broadcasted_iota(jnp.int32, (TOK, TOK), 0)
    s_ids = lax.broadcasted_iota(jnp.int32, (TOK, TOK), 1)
    lower = t_ids >= s_ids
    tri = jnp.where(lower, 1.0, 0.0).astype(BF16)
    parts = split3(jnp.concatenate([decay_ref[...], decay_ref[...]], axis=0))
    cum_rows = sum(dot(p, tri, NT) for p in parts)
    cum_cols = sum(dot(tri, p, NT) for p in parts)
    return lower, cum_rows, cum_cols


def prep_kernel(
    sk_hbm, sv_hbm, ck_hbm, cv_hbm, k_hbm, v_hbm, decay_hbm, prior_hbm,
    payload_hbm, plane_hbm,
    kv_ref, k_ref, v_ref, decay_ref, prior_ref, state_ref, sems,
):
    head = lax.axis_index("tp").astype(jnp.int32) * HEADS_DEV // GROUP_Q
    loads = begin(
        [(decay_hbm, decay_ref), (k_hbm, k_ref), (v_hbm, v_ref), (prior_hbm, prior_ref)], sems
    )
    packs = begin(
        [
            (sk_hbm.at[head], kv_ref.at[pl.ds(0, TOK), :]),
            (ck_hbm.at[head], kv_ref.at[pl.ds(TOK, CROWS), :]),
            (sv_hbm.at[head], kv_ref.at[pl.ds(KROWS, TOK), :]),
            (cv_hbm.at[head], kv_ref.at[pl.ds(KROWS + TOK, CROWS), :]),
        ],
        sems,
        4,
    )
    first = jnp.where(ctx_place() == 0, 1.0, 0.0).astype(F32)
    loads[0].wait()
    _, cum_rows, cum_cols = decay_sums(decay_ref)
    finish(packs)
    packs = begin([(kv_ref, payload_hbm), (kv_ref, plane_hbm.at[pl.ds(0, PAY), :])], sems, 8)
    finish(loads[1:])
    finals = []
    for h in range(HEADS_DEV):
        col = cum_cols[:, h : h + 1]
        final = cum_rows[h : h + 1, TOK - 1 : TOK]
        finals.append(final)
        v = v_ref[h]
        keyed_hi, keyed_lo = split2(k_ref[h].astype(F32) * jnp.exp(final - col))
        state = dot(keyed_hi, v, TN) + dot(keyed_lo, v, TN)
        state = state + (first * jnp.exp(final)) * prior_ref[h]
        state_ref[h * HD : (h + 1) * HD, :] = state.astype(BF16)
    state_ref[HEADS_DEV * HD : S_ROWS, :] = decay_lines(finals)
    stores = begin([(state_ref, plane_hbm.at[pl.ds(PAY, S_ROWS), :])], sems, 10)
    finish(packs)
    finish(stores)


def prep(*arrays):
    return run(
        prep_kernel,
        "prep",
        arrays,
        [HBM] * len(arrays),
        [((PAY, HD), BF16, HBM), ((PAY + S_ROWS, HD), BF16, HBM)],
        [
            ((PAY, HD), BF16), (LIN, BF16), (LIN, BF16), ((HEADS_DEV, TOK), F32), (STATE, F32),
            ((S_ROWS, HD), BF16),
        ],
        11,
    )


def roll_kernel(in_hbm, out_hbm, kv_ref, sems):
    z = ctx_place() // N_YC
    loads = begin([(in_hbm.at[(z + 1 + i) % N_Z], kv_ref.at[i]) for i in range(N_Z - 1)], sems)
    stores = []
    for i, load in enumerate(loads):
        load.wait()
        stores += begin([(kv_ref.at[i], out_hbm.at[i])], sems, N_Z - 1 + i)
    finish(stores)


def other_planes(column):
    shape = (N_Z - 1, PAY, HD)
    return run(
        roll_kernel,
        "other_planes",
        (column,),
        [HBM],
        [(shape, BF16, HBM)],
        [(shape, BF16)],
        2 * (N_Z - 1),
    )


def plane_scan_kernel(plane_hbm, own_hbm, own_decay_ref, total_hbm, states, own_ref, total_ref, sems):
    finish(begin([(plane_hbm.at[:, pl.ds(PAY, S_ROWS), :], states)], sems))
    place = ctx_place() % N_YC
    finals = []
    for h in range(HEADS_DEV):
        rows = slice(h * HD, (h + 1) * HD)
        acc = jnp.zeros((HD, HD), F32)
        run = jnp.zeros((1, HD), F32)
        own, own_run = acc, run
        for r in range(N_YC):
            own = jnp.where(place == r, acc, own)
            own_run = jnp.where(place == r, run, own_run)
            decay = decay_of(states[r, HEADS_DEV * HD : S_ROWS, :], h)
            acc = acc * jnp.exp(decay) + states[r, rows, :].astype(F32)
            run = run + decay
        own_ref[h] = own
        own_decay_ref[h : h + 1, :] = own_run
        total_ref[rows, :] = acc.astype(BF16)
        finals.append(run)
    total_ref[HEADS_DEV * HD : S_ROWS, :] = decay_lines(finals)
    first = (ctx_place() % N_CORE) * (HEADS_CORE * HD)
    pairs = [(own_ref, own_hbm)]
    for z in range(N_Z):
        pairs.append((total_ref.at[pl.ds(first, HEADS_CORE * HD), :], total_hbm.at[z, pl.ds(0, HEADS_CORE * HD), :]))
        pairs.append(
            (total_ref.at[pl.ds(HEADS_DEV * HD, D_ROWS), :], total_hbm.at[z, pl.ds(HEADS_CORE * HD, D_ROWS), :])
        )
    finish(begin(pairs, sems, 1))


def plane_scan(plane):
    return run(
        plane_scan_kernel,
        "plane_scan",
        (plane,),
        [HBM],
        [(STATE, F32, HBM), ((HEADS_DEV, HD), F32, VMEM), ((N_Z, U_ROWS, HD), BF16, HBM)],
        [((N_YC, S_ROWS, HD), BF16), (STATE, F32), ((S_ROWS, HD), BF16)],
        2 + 2 * N_Z,
    )


def lightning_mix_kernel(
    q_hbm, mixed_hbm, cum_hbm, own_hbm, own_decay_ref, totals_hbm, prior_hbm,
    out_hbm, square_ref,
    q_ref, mixed_ref, cum_ref, own_ref, totals_ref, prior_ref, out_ref, sems,
):
    loads = begin(
        [
            (totals_hbm, totals_ref), (own_hbm, own_ref), (prior_hbm, prior_ref),
            (cum_hbm, cum_ref), (q_hbm, q_ref), (mixed_hbm, mixed_ref),
        ],
        sems,
    )
    place = ctx_place()
    z_place = place // N_YC
    finish(loads)
    stores = []
    total = jnp.zeros((TOK, HD), F32)
    for h in range(HEADS_DEV):
        core, inner = h // HEADS_CORE, h % HEADS_CORE
        rows = slice(inner * HD, (inner + 1) * HD)
        acc = jnp.zeros((HD, HD), F32)
        for z in range(N_Z - 1):
            decay = decay_of(totals_ref[core, z, HEADS_CORE * HD : U_ROWS, :], h)
            nxt = acc * jnp.exp(decay) + totals_ref[core, z, rows, :].astype(F32)
            acc = jnp.where(z < z_place, nxt, acc)
        state = own_ref[h] + jnp.exp(own_decay_ref[h : h + 1, :]) * acc
        state = jnp.where(place == 0, prior_ref[h], state)
        hi, low = split2(state)
        q = q_ref[h]
        inter = dot(q, hi, NN) + dot(q, low, NN)
        mixed = mixed_ref[h] + jnp.exp(cum_ref[:, h : h + 1]) * inter
        out_ref[h] = mixed
        stores += begin([(out_ref.at[h], out_hbm.at[h])], sems, 6 + h)
        total = total + mixed * mixed
    ones = jnp.ones((8, HD), BF16)
    squares = sum(dot(ones, p, NT) for p in split3(total))
    for half in range(TOK // HD):
        line = squares[0:1, half * HD : (half + 1) * HD]
        square_ref[:, half, :] = jnp.broadcast_to(line, (square_ref.shape[0], HD))
    finish(stores)


def lightning_mix(n_tp, *arrays):
    specs = [HBM] * len(arrays)
    specs[4] = VMEM
    return run(
        lightning_mix_kernel,
        "lightning_mix",
        arrays,
        specs,
        [(LIN, F32, HBM), ((n_tp, TOK // HD, HD), F32, VMEM)],
        [
            (LIN, BF16), (LIN, F32), (CUM, F32), (STATE, F32),
            ((N_CORE, N_Z, U_ROWS, HD), BF16), (STATE, F32), (LIN, F32),
        ],
        6 + HEADS_DEV,
    )


def norm_kernel(count, mixed_hbm, squares_ref, gain_hbm, out_hbm, mixed_ref, gain_ref, out_ref, sems):
    finish(begin([(mixed_hbm, mixed_ref), (gain_hbm, gain_ref)], sems))
    total = jnp.sum(squares_ref[...], axis=0)
    inv = lax.rsqrt(total * (1.0 / count) + 1e-05)
    t_ids = lax.broadcasted_iota(jnp.int32, (HD, HD), 0)
    s_ids = lax.broadcasted_iota(jnp.int32, (HD, HD), 1)
    for half in range(TOK // HD):
        diag = jnp.where(t_ids == s_ids, jnp.broadcast_to(inv[half : half + 1, :], (HD, HD)), 0.0)
        col = jnp.sum(diag, axis=1, keepdims=True)
        rows = slice(half * HD, (half + 1) * HD)
        for h in range(HEADS_DEV):
            out_ref[h, rows, :] = (mixed_ref[h, rows, :] * col * gain_ref[h : h + 1, :]).astype(BF16)
    finish(begin([(out_ref, out_hbm)], sems, 2))


def lightning_norm(count, mixed, squares, gain):
    return run(
        functools.partial(norm_kernel, float(count)),
        "lightning_norm",
        (mixed, squares, gain),
        [HBM, VMEM, HBM],
        [(LIN, BF16, HBM)],
        [(LIN, F32), ((HEADS_DEV, HD), F32), (LIN, BF16)],
        3,
    )


def cache_bias(len_ref, z, r):
    lanes = lax.broadcasted_iota(jnp.int32, (1, CROWS), 1)
    return jnp.where(lanes < len_ref[z * N_YC + r], 0.0, MASK_FILL).astype(F32)


def with_ones(values):
    return jnp.concatenate([values, jnp.ones(values.shape, BF16)], axis=1)


def wide(stat, width):
    return jnp.concatenate([stat] * (width // HD), axis=1)


def near_kernel(
    scale,
    len_ref, q_hbm, plane_hbm, rest_hbm, lq_hbm, lk_hbm, lv_hbm, decay_hbm,
    m_hbm, acc_hbm, mixed_hbm, cum_hbm,
    q_ref, kv, kr, lq_ref, lk_ref, lv_ref, decay_ref, m_ref, acc_ref, mixed_ref, cum_ref, sems,
):
    loads = begin(
        [
            (decay_hbm, decay_ref), (lq_hbm, lq_ref), (lk_hbm, lk_ref), (lv_hbm, lv_ref),
            (q_hbm, q_ref), (plane_hbm.at[:, pl.ds(0, PAY), :], kv), (rest_hbm, kr),
        ],
        sems,
    )
    n_loads = len(loads)
    z = ctx_place() // N_YC
    place = ctx_place() % N_YC
    finish(loads[:4])
    lower, cum_rows, cum_cols = decay_sums(decay_ref)
    cum_ref[...] = cum_cols
    for h in range(HEADS_DEV):
        gap = jnp.where(lower, cum_cols[:, h : h + 1] - cum_rows[h : h + 1, :], 0.0)
        weights = jnp.where(lower, dot(lq_ref[h], lk_ref[h], NT) * jnp.exp(gap), 0.0).astype(BF16)
        mixed_ref[h] = dot(weights, lv_ref[h], NN)
    stores = begin([(mixed_ref, mixed_hbm), (cum_ref, cum_hbm)], sems, n_loads)

    rows = lax.broadcasted_iota(jnp.int32, (TOK, TOK), 0)
    cols = lax.broadcasted_iota(jnp.int32, (TOK, TOK), 1)
    ahead = cols - rows
    bias = [cache_bias(len_ref, z, r) for r in range(N_YC)]
    line = []
    for i in range(N_Z - 1):
        other = (z + 1 + i) % N_Z
        line.append(jnp.full((1, TOK), jnp.where(other < z, 0.0, MASK_FILL).astype(F32)))
        line.append(cache_bias(len_ref, other, place))
    line = jnp.concatenate(line, axis=1)
    finish(loads[4:])
    keys = kv[:, 0:KROWS, :].reshape(N_YC * KROWS, HD)
    values = with_ones(kv[:, KROWS:PAY, :].reshape(N_YC * KROWS, HD))
    column_keys = kr[:, 0:KROWS, :].reshape((N_Z - 1) * KROWS, HD)
    column_values = with_ones(kr[:, KROWS:PAY, :].reshape((N_Z - 1) * KROWS, HD))
    for h in range(HEADS_DEV):
        raw = dot(q_ref[h], keys, NT)
        pieces = []
        for r in range(N_YC):
            span = raw[:, r * KROWS : r * KROWS + TOK]
            pieces.append(jnp.where(ahead <= (place - r) * TOK, span, MASK_FILL))
            pieces.append(raw[:, r * KROWS + TOK : (r + 1) * KROWS] + bias[r])
        raw = jnp.concatenate(pieces, axis=1)
        column_raw = dot(q_ref[h], column_keys, NT) + line
        peak = jnp.maximum(
            jnp.max(raw, axis=1, keepdims=True), jnp.max(column_raw, axis=1, keepdims=True)
        )
        peak = jnp.broadcast_to(peak, (TOK, HD))
        probs = jnp.exp2((raw - wide(peak, raw.shape[1])) * scale).astype(BF16)
        column_probs = jnp.exp2((column_raw - wide(peak, column_raw.shape[1])) * scale).astype(BF16)
        m_ref[h] = peak
        acc_ref[h] = dot(probs, values, NN) + dot(column_probs, column_values, NN)
        stores += begin(
            [(m_ref.at[h], m_hbm.at[h]), (acc_ref.at[h], acc_hbm.at[h])], sems, n_loads + 2 + 2 * h
        )
    finish(stores)


SUMS = (HEADS_DEV, TOK, 2 * HD)


def near_work(cache_len, *arrays):
    return run(
        functools.partial(near_kernel, LOG2E / math.sqrt(HD)),
        "near_work",
        (cache_len, *arrays),
        [SMEM] + [HBM] * len(arrays),
        [(LIN, F32, HBM), (SUMS, F32, HBM), (LIN, F32, HBM), (CUM, F32, HBM)],
        [
            (LIN, BF16), ((N_YC, PAY, HD), BF16), ((N_Z - 1, PAY, HD), BF16),
            (LIN, BF16), (LIN, BF16), (LIN, BF16), ((HEADS_DEV, TOK), F32),
            (LIN, F32), (SUMS, F32), (LIN, F32), (CUM, F32),
        ],
        9 + 2 * HEADS_DEV,
    )


def far_kernel(
    scale, len_ref, q_hbm, m_hbm, acc_hbm, kv_hbm, out_hbm, q_ref, m_ref, acc_ref, kv, out_ref, sems
):
    z_place = ctx_place() // N_YC
    place = ctx_place() % N_YC
    others = [(place + 1 + j) % N_YC for j in range(N_FAR)]
    loads = begin([(q_hbm, q_ref), (m_hbm, m_ref), (acc_hbm, acc_ref)], sems)
    blocks = []
    for i in range(N_Z - 1):
        pairs = [(kv_hbm.at[r, i], kv.at[i, j]) for j, r in enumerate(others)]
        blocks.append(begin(pairs, sems, 3 + i * N_FAR))
    finish(loads)

    def update(h, raw, values):
        m_old = m_ref[h]
        m_new = jnp.maximum(m_old, jnp.max(raw, axis=1, keepdims=True))
        probs = jnp.exp2((raw - wide(m_new, raw.shape[1])) * scale)
        alpha = jnp.exp2((m_old - m_new) * scale)
        m_ref[h] = m_new
        acc_ref[h] = acc_ref[h] * wide(alpha, 2 * HD) + dot(probs.astype(BF16), values, NN)

    for i in range(N_Z - 1):
        finish(blocks[i])
        z = (z_place + 1 + i) % N_Z
        bias = [cache_bias(len_ref, z, r) for r in others]

        @pl.when(z < z_place)
        def whole():
            keys = kv[i, :, 0:KROWS, :].reshape(N_FAR * KROWS, HD)
            values = with_ones(kv[i, :, KROWS:PAY, :].reshape(N_FAR * KROWS, HD))
            for h in range(HEADS_DEV):
                raw = dot(q_ref[h], keys, NT)
                pieces = []
                for r in range(N_FAR):
                    pieces.append(raw[:, r * KROWS : r * KROWS + TOK])
                    pieces.append(raw[:, r * KROWS + TOK : (r + 1) * KROWS] + bias[r])
                update(h, jnp.concatenate(pieces, axis=1), values)

        @pl.when(z > z_place)
        def cache_only():
            keys = kv[i, :, TOK:KROWS, :].reshape(N_FAR * CROWS, HD)
            values = with_ones(kv[i, :, KROWS + TOK : PAY, :].reshape(N_FAR * CROWS, HD))
            line = jnp.concatenate(bias, axis=1)
            for h in range(HEADS_DEV):
                update(h, dot(q_ref[h], keys, NT) + line, values)

    stores = []
    for h in range(HEADS_DEV):
        acc = acc_ref[h]
        out_ref[h] = (acc[:, 0:HD] / acc[:, HD : 2 * HD]).astype(BF16)
        stores += begin([(out_ref.at[h], out_hbm.at[h])], sems, 3 + (N_Z - 1) * N_FAR + h)
    finish(stores)


def far_attention(cache_len, soft_q, peaks, sums, kv):
    return run(
        functools.partial(far_kernel, LOG2E / math.sqrt(HD)),
        "far_attention",
        (cache_len, soft_q, peaks, sums, kv),
        [SMEM] + [HBM] * 4,
        [(LIN, BF16, HBM)],
        [(LIN, BF16), (LIN, F32), (SUMS, F32), ((N_Z - 1, N_FAR, PAY, HD), BF16), (LIN, BF16)],
        3 + (N_Z - 1) * N_FAR + HEADS_DEV,
    )


def per_device(
    lin_q,
    lin_k,
    lin_v,
    log_decay,
    prior_state,
    lin_gain,
    soft_q,
    span_k,
    span_v,
    cache_k,
    cached_value_rows,
    cache_len,
):
    payload, plane_payload = prep(
        span_k, span_v, cache_k, cached_value_rows, lin_k, lin_v, log_decay, prior_state
    )
    plane = lax.all_gather(plane_payload, "ctx", axis=0, tiled=True, axis_index_groups=YC_GROUPS)
    plane = plane.reshape(N_YC, PAY + S_ROWS, HD)
    column = lax.all_gather(payload, "ctx", axis=0, tiled=True, axis_index_groups=Z_GROUPS)
    rest = other_planes(column.reshape(N_Z, PAY, HD))
    far = lax.all_gather(
        rest.reshape((N_Z - 1) * PAY, HD), "ctx", axis=0, tiled=True, axis_index_groups=YC_GROUPS
    )
    far = far.reshape(N_YC, N_Z - 1, PAY, HD)

    own, own_decay, plane_totals = plane_scan(plane)
    totals = lax.all_to_all(plane_totals, "ctx", 0, 0, axis_index_groups=Z_GROUPS)
    totals = lax.all_gather(totals, "ctx", axis=0, axis_index_groups=CORE_GROUPS)
    peaks, sums, mixed, cum = near_work(
        cache_len, soft_q, plane, rest, lin_q, lin_k, lin_v, log_decay
    )
    own, peaks = lax.optimization_barrier((own, peaks))
    n_tp = lax.axis_size("tp")
    mixed, squares = lightning_mix(
        n_tp, lin_q, mixed, cum, own, own_decay, totals, prior_state
    )
    squares, peaks = lax.optimization_barrier((squares, peaks))
    all_squares = lax.all_to_all(squares, "tp", 0, 0)
    soft_out = far_attention(cache_len, soft_q, peaks, sums, far)
    mixed, soft_out = lax.optimization_barrier((mixed, soft_out))
    normalized = lightning_norm(n_tp * HEADS_DEV * HD, mixed, all_squares, lin_gain)
    return (normalized, soft_out)


def solution(mesh):
    placed = (
        P("tp", "ctx", None),
        P("tp", "ctx", None),
        P("tp", "ctx", None),
        P("tp", "ctx"),
        P("tp", None, None),
        P("tp", None),
        P("tp", "ctx", None),
        P(None, "ctx", None),
        P(None, "ctx", None),
        P(None, "ctx", None),
        P(None, "ctx", None),
        P(),
    )
    return jax.shard_map(
        per_device,
        mesh=mesh,
        in_specs=placed,
        out_specs=(P("tp", "ctx", None), P("tp", "ctx", None)),
        check_vma=False,
    )
```

```python
import functools
import math

import jax
import jax.numpy as jnp
from jax import lax
from jax.experimental import pallas as pl
from jax.experimental.pallas import tpu as pltpu
from jax.sharding import PartitionSpec as P

GROUP_Q = 8
N_Z, N_Y, N_CORE = 4, 4, 2
N_CTX = N_Z * N_Y * N_CORE
N_YC = N_Y * N_CORE
N_FAR = N_YC - 1
HD = 128
HEADS_DEV = 4
TOK = 256
CROWS = 128
KROWS = TOK + CROWS
PAY = 2 * KROWS
D_ROWS = 16
S_ROWS = HEADS_DEV * HD + D_ROWS
HEADS_CORE = HEADS_DEV // N_CORE
U_ROWS = HEADS_CORE * HD + D_ROWS
MASK_FILL = -1e30
LOG2E = 1.4426950408889634
VMEM_LIMIT = 60 * 1024 * 1024

F32 = jnp.float32
BF16 = jnp.bfloat16

Z_GROUPS = [[z * N_YC + r for z in range(N_Z)] for r in range(N_YC)]
YC_GROUPS = [[z * N_YC + r for r in range(N_YC)] for z in range(N_Z)]
CORE_GROUPS = [[N_CORE * r + i for i in range(N_CORE)] for r in range(N_CTX // N_CORE)]

NT = (((1,), (1,)), ((), ()))
NN = (((1,), (0,)), ((), ()))
TN = (((0,), (0,)), ((), ()))


def dot(a, b, dims):
    return lax.dot_general(a, b, dims, preferred_element_type=F32)


def split3(x):
    hi = x.astype(BF16)
    rest = x - hi.astype(F32)
    mid = rest.astype(BF16)
    low = (rest - mid.astype(F32)).astype(BF16)
    return hi, mid, low


def split2(x):
    hi = x.astype(BF16)
    return hi, (x - hi.astype(F32)).astype(BF16)


HBM = pl.BlockSpec(memory_space=pltpu.HBM)
VMEM = pl.BlockSpec(memory_space=pltpu.VMEM)
SMEM = pl.BlockSpec(memory_space=pltpu.SMEM)
LIN = (HEADS_DEV, TOK, HD)
STATE = (HEADS_DEV, HD, HD)
CUM = (TOK, 2 * HEADS_DEV)


def ctx_place():
    return lax.axis_index("ctx").astype(jnp.int32)


def begin(pairs, sems, base=0):
    copies = [pltpu.make_async_copy(a, b, sems.at[base + i]) for i, (a, b) in enumerate(pairs)]
    for copy in copies:
        copy.start()
    return copies


def finish(copies):
    for copy in copies:
        copy.wait()


def run(kernel, name, operands, in_specs, outs, scratch, n_sems):
    single = len(outs) == 1
    shapes = tuple(jax.ShapeDtypeStruct(shape, kind) for shape, kind, _ in outs)
    specs = tuple(spec for _, _, spec in outs)
    return pl.pallas_call(
        kernel,
        out_shape=shapes[0] if single else shapes,
        in_specs=in_specs,
        out_specs=specs[0] if single else specs,
        scratch_shapes=[pltpu.VMEM(shape, kind) for shape, kind in scratch]
        + [pltpu.SemaphoreType.DMA((n_sems,))],
        compiler_params=pltpu.CompilerParams(vmem_limit_bytes=VMEM_LIMIT),
        name=name,
    )(*operands)


def decay_lines(values):
    ids = lax.broadcasted_iota(jnp.int32, (D_ROWS, HD), 0)
    lines = jnp.zeros((D_ROWS, HD), F32)
    for h, value in enumerate(values):
        for i, part in enumerate(split3(jnp.broadcast_to(value, (1, HD)))):
            lines = jnp.where(ids == 3 * h + i, part.astype(F32), lines)
    return lines.astype(BF16)


def decay_of(lines, h):
    lines = lines[3 * h : 3 * h + 3].astype(F32)
    return lines[0:1] + lines[1:2] + lines[2:3]


def decay_sums(decay_ref):
    t_ids = lax.broadcasted_iota(jnp.int32, (TOK, TOK), 0)
    s_ids = lax.broadcasted_iota(jnp.int32, (TOK, TOK), 1)
    lower = t_ids >= s_ids
    tri = jnp.where(lower, 1.0, 0.0).astype(BF16)
    parts = split3(jnp.concatenate([decay_ref[...], decay_ref[...]], axis=0))
    cum_rows = sum(dot(p, tri, NT) for p in parts)
    cum_cols = sum(dot(tri, p, NT) for p in parts)
    return lower, cum_rows, cum_cols


def prep_kernel(
    sk_hbm, sv_hbm, ck_hbm, cv_hbm, k_hbm, v_hbm, decay_hbm, prior_hbm,
    payload_hbm, plane_hbm,
    kv_ref, k_ref, v_ref, decay_ref, prior_ref, state_ref, sems,
):
    head = lax.axis_index("tp").astype(jnp.int32) * HEADS_DEV // GROUP_Q
    loads = begin(
        [(decay_hbm, decay_ref), (k_hbm, k_ref), (v_hbm, v_ref), (prior_hbm, prior_ref)], sems
    )
    packs = begin(
        [
            (sk_hbm.at[head], kv_ref.at[pl.ds(0, TOK), :]),
            (ck_hbm.at[head], kv_ref.at[pl.ds(TOK, CROWS), :]),
            (sv_hbm.at[head], kv_ref.at[pl.ds(KROWS, TOK), :]),
            (cv_hbm.at[head], kv_ref.at[pl.ds(KROWS + TOK, CROWS), :]),
        ],
        sems,
        4,
    )
    first = jnp.where(ctx_place() == 0, 1.0, 0.0).astype(F32)
    loads[0].wait()
    _, cum_rows, cum_cols = decay_sums(decay_ref)
    finish(packs)
    packs = begin([(kv_ref, payload_hbm), (kv_ref, plane_hbm.at[pl.ds(0, PAY), :])], sems, 8)
    finish(loads[1:])
    finals = []
    for h in range(HEADS_DEV):
        col = cum_cols[:, h : h + 1]
        final = cum_rows[h : h + 1, TOK - 1 : TOK]
        finals.append(final)
        v = v_ref[h]
        keyed_hi, keyed_lo = split2(k_ref[h].astype(F32) * jnp.exp(final - col))
        state = dot(keyed_hi, v, TN) + dot(keyed_lo, v, TN)
        state = state + (first * jnp.exp(final)) * prior_ref[h]
        state_ref[h * HD : (h + 1) * HD, :] = state.astype(BF16)
    state_ref[HEADS_DEV * HD : S_ROWS, :] = decay_lines(finals)
    stores = begin([(state_ref, plane_hbm.at[pl.ds(PAY, S_ROWS), :])], sems, 10)
    finish(packs)
    finish(stores)


def prep(*arrays):
    return run(
        prep_kernel,
        "prep",
        arrays,
        [HBM] * len(arrays),
        [((PAY, HD), BF16, HBM), ((PAY + S_ROWS, HD), BF16, HBM)],
        [
            ((PAY, HD), BF16), (LIN, BF16), (LIN, BF16), ((HEADS_DEV, TOK), F32), (STATE, F32),
            ((S_ROWS, HD), BF16),
        ],
        11,
    )


def roll_kernel(in_hbm, out_hbm, kv_ref, sems):
    z = ctx_place() // N_YC
    loads = begin([(in_hbm.at[(z + 1 + i) % N_Z], kv_ref.at[i]) for i in range(N_Z - 1)], sems)
    stores = []
    for i, load in enumerate(loads):
        load.wait()
        stores += begin([(kv_ref.at[i], out_hbm.at[i])], sems, N_Z - 1 + i)
    finish(stores)


def other_planes(column):
    shape = (N_Z - 1, PAY, HD)
    return run(
        roll_kernel,
        "other_planes",
        (column,),
        [HBM],
        [(shape, BF16, HBM)],
        [(shape, BF16)],
        2 * (N_Z - 1),
    )


def plane_scan_kernel(plane_hbm, own_hbm, own_decay_ref, total_hbm, states, own_ref, total_ref, sems):
    finish(begin([(plane_hbm.at[:, pl.ds(PAY, S_ROWS), :], states)], sems))
    place = ctx_place() % N_YC
    finals = []
    for h in range(HEADS_DEV):
        rows = slice(h * HD, (h + 1) * HD)
        acc = jnp.zeros((HD, HD), F32)
        run = jnp.zeros((1, HD), F32)
        own, own_run = acc, run
        for r in range(N_YC):
            own = jnp.where(place == r, acc, own)
            own_run = jnp.where(place == r, run, own_run)
            decay = decay_of(states[r, HEADS_DEV * HD : S_ROWS, :], h)
            acc = acc * jnp.exp(decay) + states[r, rows, :].astype(F32)
            run = run + decay
        own_ref[h] = own
        own_decay_ref[h : h + 1, :] = own_run
        total_ref[rows, :] = acc.astype(BF16)
        finals.append(run)
    total_ref[HEADS_DEV * HD : S_ROWS, :] = decay_lines(finals)
    first = (ctx_place() % N_CORE) * (HEADS_CORE * HD)
    pairs = [(own_ref, own_hbm)]
    for z in range(N_Z):
        pairs.append((total_ref.at[pl.ds(first, HEADS_CORE * HD), :], total_hbm.at[z, pl.ds(0, HEADS_CORE * HD), :]))
        pairs.append(
            (total_ref.at[pl.ds(HEADS_DEV * HD, D_ROWS), :], total_hbm.at[z, pl.ds(HEADS_CORE * HD, D_ROWS), :])
        )
    finish(begin(pairs, sems, 1))


def plane_scan(plane):
    return run(
        plane_scan_kernel,
        "plane_scan",
        (plane,),
        [HBM],
        [(STATE, F32, HBM), ((HEADS_DEV, HD), F32, VMEM), ((N_Z, U_ROWS, HD), BF16, HBM)],
        [((N_YC, S_ROWS, HD), BF16), (STATE, F32), ((S_ROWS, HD), BF16)],
        2 + 2 * N_Z,
    )


def lightning_mix_kernel(
    q_hbm, mixed_hbm, cum_hbm, own_hbm, own_decay_ref, totals_hbm, prior_hbm,
    out_hbm, square_ref,
    q_ref, mixed_ref, cum_ref, own_ref, totals_ref, prior_ref, out_ref, sems,
):
    loads = begin(
        [
            (totals_hbm, totals_ref), (own_hbm, own_ref), (prior_hbm, prior_ref),
            (cum_hbm, cum_ref), (q_hbm, q_ref), (mixed_hbm, mixed_ref),
        ],
        sems,
    )
    place = ctx_place()
    z_place = place // N_YC
    finish(loads)
    stores = []
    total = jnp.zeros((TOK, HD), F32)
    for h in range(HEADS_DEV):
        core, inner = h // HEADS_CORE, h % HEADS_CORE
        rows = slice(inner * HD, (inner + 1) * HD)
        acc = jnp.zeros((HD, HD), F32)
        for z in range(N_Z - 1):
            decay = decay_of(totals_ref[core, z, HEADS_CORE * HD : U_ROWS, :], h)
            nxt = acc * jnp.exp(decay) + totals_ref[core, z, rows, :].astype(F32)
            acc = jnp.where(z < z_place, nxt, acc)
        state = own_ref[h] + jnp.exp(own_decay_ref[h : h + 1, :]) * acc
        state = jnp.where(place == 0, prior_ref[h], state)
        hi, low = split2(state)
        q = q_ref[h]
        inter = dot(q, hi, NN) + dot(q, low, NN)
        mixed = mixed_ref[h] + jnp.exp(cum_ref[:, h : h + 1]) * inter
        out_ref[h] = mixed
        stores += begin([(out_ref.at[h], out_hbm.at[h])], sems, 6 + h)
        total = total + mixed * mixed
    ones = jnp.ones((8, HD), BF16)
    squares = sum(dot(ones, p, NT) for p in split3(total))
    for half in range(TOK // HD):
        line = squares[0:1, half * HD : (half + 1) * HD]
        square_ref[:, half, :] = jnp.broadcast_to(line, (square_ref.shape[0], HD))
    finish(stores)


def lightning_mix(n_tp, *arrays):
    specs = [HBM] * len(arrays)
    specs[4] = VMEM
    return run(
        lightning_mix_kernel,
        "lightning_mix",
        arrays,
        specs,
        [(LIN, F32, HBM), ((n_tp, TOK // HD, HD), F32, VMEM)],
        [
            (LIN, BF16), (LIN, F32), (CUM, F32), (STATE, F32),
            ((N_CORE, N_Z, U_ROWS, HD), BF16), (STATE, F32), (LIN, F32),
        ],
        6 + HEADS_DEV,
    )


def norm_kernel(count, mixed_hbm, squares_ref, gain_hbm, out_hbm, mixed_ref, gain_ref, out_ref, sems):
    loads = begin([(gain_hbm, gain_ref)] + [(mixed_hbm.at[h], mixed_ref.at[h]) for h in range(HEADS_DEV)], sems)
    total = jnp.sum(squares_ref[...], axis=0)
    inv = lax.rsqrt(total * (1.0 / count) + 1e-05)
    t_ids = lax.broadcasted_iota(jnp.int32, (HD, HD), 0)
    s_ids = lax.broadcasted_iota(jnp.int32, (HD, HD), 1)
    factors = []
    for half in range(TOK // HD):
        diag = jnp.where(t_ids == s_ids, jnp.broadcast_to(inv[half : half + 1, :], (HD, HD)), 0.0)
        factors.append(jnp.broadcast_to(jnp.sum(diag, axis=1, keepdims=True), (HD, HD)))
    factor = jnp.concatenate(factors, axis=0)
    loads[0].wait()
    stores = []
    for h in range(HEADS_DEV):
        loads[1 + h].wait()
        out_ref[h] = (mixed_ref[h] * factor * gain_ref[h : h + 1, :]).astype(BF16)
        stores += begin([(out_ref.at[h], out_hbm.at[h])], sems, 1 + HEADS_DEV + h)
    finish(stores)


def lightning_norm(count, mixed, squares, gain):
    return run(
        functools.partial(norm_kernel, float(count)),
        "lightning_norm",
        (mixed, squares, gain),
        [HBM, VMEM, HBM],
        [(LIN, BF16, HBM)],
        [(LIN, F32), ((HEADS_DEV, HD), F32), (LIN, BF16)],
        1 + 2 * HEADS_DEV,
    )


def cache_bias(len_ref, z, r):
    lanes = lax.broadcasted_iota(jnp.int32, (1, CROWS), 1)
    return jnp.where(lanes < len_ref[z * N_YC + r], 0.0, MASK_FILL).astype(F32)


def with_ones(values):
    return jnp.concatenate([values, jnp.ones(values.shape, BF16)], axis=1)


def wide(stat, width):
    return jnp.concatenate([stat] * (width // HD), axis=1)


def by_head(score, soften, fold):
    ahead, held = score(0), None
    for h in range(HEADS_DEV + 1):
        fresh = None
        if h < HEADS_DEV:
            raw = ahead
            if h + 1 < HEADS_DEV:
                ahead = score(h + 1)
            fresh = soften(h, raw)
        if held is not None:
            fold(h - 1, held)
        held = fresh


def near_kernel(
    scale,
    len_ref, q_hbm, plane_hbm, rest_hbm, lq_hbm, lk_hbm, lv_hbm, decay_hbm,
    m_hbm, acc_hbm, mixed_hbm, cum_hbm,
    q_ref, kv, kr, lq_ref, lk_ref, lv_ref, decay_ref, m_ref, acc_ref, mixed_ref, cum_ref, sems,
):
    loads = begin(
        [
            (decay_hbm, decay_ref), (lq_hbm, lq_ref), (lk_hbm, lk_ref), (lv_hbm, lv_ref),
            (q_hbm, q_ref), (plane_hbm.at[:, pl.ds(0, PAY), :], kv), (rest_hbm, kr),
        ],
        sems,
    )
    n_loads = len(loads)
    z = ctx_place() // N_YC
    place = ctx_place() % N_YC
    finish(loads[:4])
    lower, cum_rows, cum_cols = decay_sums(decay_ref)
    cum_ref[...] = cum_cols
    for h in range(HEADS_DEV):
        gap = jnp.where(lower, cum_cols[:, h : h + 1] - cum_rows[h : h + 1, :], 0.0)
        weights = jnp.where(lower, dot(lq_ref[h], lk_ref[h], NT) * jnp.exp(gap), 0.0).astype(BF16)
        mixed_ref[h] = dot(weights, lv_ref[h], NN)
    stores = begin([(mixed_ref, mixed_hbm), (cum_ref, cum_hbm)], sems, n_loads)

    rows = lax.broadcasted_iota(jnp.int32, (TOK, TOK), 0)
    cols = lax.broadcasted_iota(jnp.int32, (TOK, TOK), 1)
    ahead = cols - rows
    bias = [cache_bias(len_ref, z, r) for r in range(N_YC)]
    line = []
    for i in range(N_Z - 1):
        other = (z + 1 + i) % N_Z
        line.append(jnp.full((1, TOK), jnp.where(other < z, 0.0, MASK_FILL).astype(F32)))
        line.append(cache_bias(len_ref, other, place))
    line = jnp.concatenate(line, axis=1)
    finish(loads[4:])
    keys = kv[:, 0:KROWS, :].reshape(N_YC * KROWS, HD)
    values = with_ones(kv[:, KROWS:PAY, :].reshape(N_YC * KROWS, HD))
    column_keys = kr[:, 0:KROWS, :].reshape((N_Z - 1) * KROWS, HD)
    column_values = with_ones(kr[:, KROWS:PAY, :].reshape((N_Z - 1) * KROWS, HD))

    def score(h):
        return dot(q_ref[h], keys, NT), dot(q_ref[h], column_keys, NT)

    def soften(h, raws):
        raw, column_raw = raws
        pieces = []
        for r in range(N_YC):
            span = raw[:, r * KROWS : r * KROWS + TOK]
            pieces.append(jnp.where(ahead <= (place - r) * TOK, span, MASK_FILL))
            pieces.append(raw[:, r * KROWS + TOK : (r + 1) * KROWS] + bias[r])
        raw = jnp.concatenate(pieces, axis=1)
        column_raw = column_raw + line
        peak = jnp.maximum(
            jnp.max(raw, axis=1, keepdims=True), jnp.max(column_raw, axis=1, keepdims=True)
        )
        peak = jnp.broadcast_to(peak, (TOK, HD))
        m_ref[h] = peak
        probs = jnp.exp2((raw - wide(peak, raw.shape[1])) * scale).astype(BF16)
        column_probs = jnp.exp2((column_raw - wide(peak, column_raw.shape[1])) * scale).astype(BF16)
        return probs, column_probs

    def fold(h, probs):
        acc_ref[h] = dot(probs[0], values, NN) + dot(probs[1], column_values, NN)
        stores.extend(
            begin([(m_ref.at[h], m_hbm.at[h]), (acc_ref.at[h], acc_hbm.at[h])], sems, n_loads + 2 + 2 * h)
        )

    by_head(score, soften, fold)
    finish(stores)


SUMS = (HEADS_DEV, TOK, 2 * HD)


def near_work(cache_len, *arrays):
    return run(
        functools.partial(near_kernel, LOG2E / math.sqrt(HD)),
        "near_work",
        (cache_len, *arrays),
        [SMEM] + [HBM] * len(arrays),
        [(LIN, F32, HBM), (SUMS, F32, HBM), (LIN, F32, HBM), (CUM, F32, HBM)],
        [
            (LIN, BF16), ((N_YC, PAY, HD), BF16), ((N_Z - 1, PAY, HD), BF16),
            (LIN, BF16), (LIN, BF16), (LIN, BF16), ((HEADS_DEV, TOK), F32),
            (LIN, F32), (SUMS, F32), (LIN, F32), (CUM, F32),
        ],
        9 + 2 * HEADS_DEV,
    )


def far_kernel(
    scale, len_ref, q_hbm, m_hbm, acc_hbm, kv_hbm, out_hbm, q_ref, m_ref, acc_ref, kv, out_ref, sems
):
    z_place = ctx_place() // N_YC
    place = ctx_place() % N_YC
    others = [(place + 1 + j) % N_YC for j in range(N_FAR)]
    loads = begin([(q_hbm, q_ref), (m_hbm, m_ref), (acc_hbm, acc_ref)], sems)

    def shards(i):
        pairs = [(kv_hbm.at[r, i], kv.at[i, j]) for j, r in enumerate(others)]
        return begin(pairs, sems, 3 + i * N_FAR)

    blocks = [shards(0)]
    finish(loads)
    finish(blocks[0])
    blocks += [shards(i) for i in range(1, N_Z - 1)]

    def update(keys, values, mask):
        def score(h):
            return dot(q_ref[h], keys, NT)

        def soften(h, raw):
            raw = mask(raw)
            m_old = m_ref[h]
            m_new = jnp.maximum(m_old, jnp.max(raw, axis=1, keepdims=True))
            m_ref[h] = m_new
            probs = jnp.exp2((raw - wide(m_new, raw.shape[1])) * scale).astype(BF16)
            return probs, jnp.exp2((m_old - m_new) * scale)

        def fold(h, held):
            probs, alpha = held
            acc_ref[h] = acc_ref[h] * wide(alpha, 2 * HD) + dot(probs, values, NN)

        by_head(score, soften, fold)

    for i in range(N_Z - 1):
        if i > 0:
            finish(blocks[i])
        z = (z_place + 1 + i) % N_Z
        bias = [cache_bias(len_ref, z, r) for r in others]

        @pl.when(z < z_place)
        def whole():
            keys = kv[i, :, 0:KROWS, :].reshape(N_FAR * KROWS, HD)
            values = with_ones(kv[i, :, KROWS:PAY, :].reshape(N_FAR * KROWS, HD))

            def mask(raw):
                pieces = []
                for r in range(N_FAR):
                    pieces.append(raw[:, r * KROWS : r * KROWS + TOK])
                    pieces.append(raw[:, r * KROWS + TOK : (r + 1) * KROWS] + bias[r])
                return jnp.concatenate(pieces, axis=1)

            update(keys, values, mask)

        @pl.when(z > z_place)
        def cache_only():
            keys = kv[i, :, TOK:KROWS, :].reshape(N_FAR * CROWS, HD)
            values = with_ones(kv[i, :, KROWS + TOK : PAY, :].reshape(N_FAR * CROWS, HD))
            line = jnp.concatenate(bias, axis=1)
            update(keys, values, lambda raw: raw + line)

    stores = []
    for h in range(HEADS_DEV):
        acc = acc_ref[h]
        out_ref[h] = (acc[:, 0:HD] / acc[:, HD : 2 * HD]).astype(BF16)
        stores += begin([(out_ref.at[h], out_hbm.at[h])], sems, 3 + (N_Z - 1) * N_FAR + h)
    finish(stores)


def far_attention(cache_len, soft_q, peaks, sums, kv):
    return run(
        functools.partial(far_kernel, LOG2E / math.sqrt(HD)),
        "far_attention",
        (cache_len, soft_q, peaks, sums, kv),
        [SMEM] + [HBM] * 4,
        [(LIN, BF16, HBM)],
        [(LIN, BF16), (LIN, F32), (SUMS, F32), ((N_Z - 1, N_FAR, PAY, HD), BF16), (LIN, BF16)],
        3 + (N_Z - 1) * N_FAR + HEADS_DEV,
    )


def per_device(
    lin_q,
    lin_k,
    lin_v,
    log_decay,
    prior_state,
    lin_gain,
    soft_q,
    span_k,
    span_v,
    cache_k,
    cached_value_rows,
    cache_len,
):
    payload, plane_payload = prep(
        span_k, span_v, cache_k, cached_value_rows, lin_k, lin_v, log_decay, prior_state
    )
    plane = lax.all_gather(plane_payload, "ctx", axis=0, tiled=True, axis_index_groups=YC_GROUPS)
    plane = plane.reshape(N_YC, PAY + S_ROWS, HD)
    column = lax.all_gather(payload, "ctx", axis=0, tiled=True, axis_index_groups=Z_GROUPS)
    rest = other_planes(column.reshape(N_Z, PAY, HD))
    far = lax.all_gather(
        rest.reshape((N_Z - 1) * PAY, HD), "ctx", axis=0, tiled=True, axis_index_groups=YC_GROUPS
    )
    far = far.reshape(N_YC, N_Z - 1, PAY, HD)

    own, own_decay, plane_totals = plane_scan(plane)
    totals = lax.all_to_all(plane_totals, "ctx", 0, 0, axis_index_groups=Z_GROUPS)
    totals = lax.all_gather(totals, "ctx", axis=0, axis_index_groups=CORE_GROUPS)
    peaks, sums, mixed, cum = near_work(
        cache_len, soft_q, plane, rest, lin_q, lin_k, lin_v, log_decay
    )
    own, peaks = lax.optimization_barrier((own, peaks))
    n_tp = lax.axis_size("tp")
    mixed, squares = lightning_mix(
        n_tp, lin_q, mixed, cum, own, own_decay, totals, prior_state
    )
    squares, peaks = lax.optimization_barrier((squares, peaks))
    all_squares = lax.all_to_all(squares, "tp", 0, 0)
    soft_out = far_attention(cache_len, soft_q, peaks, sums, far)
    mixed, soft_out = lax.optimization_barrier((mixed, soft_out))
    normalized = lightning_norm(n_tp * HEADS_DEV * HD, mixed, all_squares, lin_gain)
    return (normalized, soft_out)


def solution(mesh):
    placed = (
        P("tp", "ctx", None),
        P("tp", "ctx", None),
        P("tp", "ctx", None),
        P("tp", "ctx"),
        P("tp", None, None),
        P("tp", None),
        P("tp", "ctx", None),
        P(None, "ctx", None),
        P(None, "ctx", None),
        P(None, "ctx", None),
        P(None, "ctx", None),
        P(),
    )
    return jax.shard_map(
        per_device,
        mesh=mesh,
        in_specs=placed,
        out_specs=(P("tp", "ctx", None), P("tp", "ctx", None)),
        check_vma=False,
    )
```

```python
import functools
import math

import jax
import jax.numpy as jnp
from jax import lax
from jax.experimental import pallas as pl
from jax.experimental.pallas import tpu as pltpu
from jax.sharding import PartitionSpec as P

GROUP_Q = 8
N_Z, N_Y, N_CORE = 4, 4, 2
N_CTX = N_Z * N_Y * N_CORE
N_YC = N_Y * N_CORE
N_FAR = N_YC - 1
HD = 128
HEADS_DEV = 4
TOK = 256
CROWS = 128
KROWS = TOK + CROWS
PAY = 2 * KROWS
D_ROWS = 16
S_ROWS = HEADS_DEV * HD + D_ROWS
HEADS_CORE = HEADS_DEV // N_CORE
U_ROWS = HEADS_CORE * HD + D_ROWS
MASK_FILL = -1e30
LOG2E = 1.4426950408889634
VMEM_LIMIT = 60 * 1024 * 1024

F32 = jnp.float32
BF16 = jnp.bfloat16

Z_GROUPS = [[z * N_YC + r for z in range(N_Z)] for r in range(N_YC)]
YC_GROUPS = [[z * N_YC + r for r in range(N_YC)] for z in range(N_Z)]
CORE_GROUPS = [[N_CORE * r + i for i in range(N_CORE)] for r in range(N_CTX // N_CORE)]

NT = (((1,), (1,)), ((), ()))
NN = (((1,), (0,)), ((), ()))
TN = (((0,), (0,)), ((), ()))


def dot(a, b, dims):
    return lax.dot_general(a, b, dims, preferred_element_type=F32)


def split3(x):
    hi = x.astype(BF16)
    rest = x - hi.astype(F32)
    mid = rest.astype(BF16)
    low = (rest - mid.astype(F32)).astype(BF16)
    return hi, mid, low


def split2(x):
    hi = x.astype(BF16)
    return hi, (x - hi.astype(F32)).astype(BF16)


HBM = pl.BlockSpec(memory_space=pltpu.HBM)
VMEM = pl.BlockSpec(memory_space=pltpu.VMEM)
SMEM = pl.BlockSpec(memory_space=pltpu.SMEM)
LIN = (HEADS_DEV, TOK, HD)
STATE = (HEADS_DEV, HD, HD)
CUM = (TOK, 2 * HEADS_DEV)


def ctx_place():
    return lax.axis_index("ctx").astype(jnp.int32)


def begin(pairs, sems, base=0):
    copies = [pltpu.make_async_copy(a, b, sems.at[base + i]) for i, (a, b) in enumerate(pairs)]
    for copy in copies:
        copy.start()
    return copies


def finish(copies):
    for copy in copies:
        copy.wait()


def run(kernel, name, operands, in_specs, outs, scratch, n_sems):
    single = len(outs) == 1
    shapes = tuple(jax.ShapeDtypeStruct(shape, kind) for shape, kind, _ in outs)
    specs = tuple(spec for _, _, spec in outs)
    return pl.pallas_call(
        kernel,
        out_shape=shapes[0] if single else shapes,
        in_specs=in_specs,
        out_specs=specs[0] if single else specs,
        scratch_shapes=[pltpu.VMEM(shape, kind) for shape, kind in scratch]
        + [pltpu.SemaphoreType.DMA((n_sems,))],
        compiler_params=pltpu.CompilerParams(vmem_limit_bytes=VMEM_LIMIT),
        name=name,
    )(*operands)


def decay_lines(values):
    ids = lax.broadcasted_iota(jnp.int32, (D_ROWS, HD), 0)
    lines = jnp.zeros((D_ROWS, HD), F32)
    for h, value in enumerate(values):
        for i, part in enumerate(split3(jnp.broadcast_to(value, (1, HD)))):
            lines = jnp.where(ids == 3 * h + i, part.astype(F32), lines)
    return lines.astype(BF16)


def decay_of(lines, h):
    lines = lines[3 * h : 3 * h + 3].astype(F32)
    return lines[0:1] + lines[1:2] + lines[2:3]


def decay_sums(decay_ref):
    t_ids = lax.broadcasted_iota(jnp.int32, (TOK, TOK), 0)
    s_ids = lax.broadcasted_iota(jnp.int32, (TOK, TOK), 1)
    lower = t_ids >= s_ids
    tri = jnp.where(lower, 1.0, 0.0).astype(BF16)
    parts = split3(jnp.concatenate([decay_ref[...], decay_ref[...]], axis=0))
    cum_rows = sum(dot(p, tri, NT) for p in parts)
    cum_cols = sum(dot(tri, p, NT) for p in parts)
    return lower, cum_rows, cum_cols


def prep_kernel(
    sk_hbm, sv_hbm, ck_hbm, cv_hbm, k_hbm, v_hbm, decay_hbm, prior_hbm,
    payload_hbm, plane_hbm,
    kv_ref, k_ref, v_ref, decay_ref, prior_ref, state_ref, sems,
):
    head = lax.axis_index("tp").astype(jnp.int32) * HEADS_DEV // GROUP_Q
    loads = begin(
        [(decay_hbm, decay_ref), (k_hbm, k_ref), (v_hbm, v_ref), (prior_hbm, prior_ref)], sems
    )
    packs = begin(
        [
            (sk_hbm.at[head], kv_ref.at[pl.ds(0, TOK), :]),
            (ck_hbm.at[head], kv_ref.at[pl.ds(TOK, CROWS), :]),
            (sv_hbm.at[head], kv_ref.at[pl.ds(KROWS, TOK), :]),
            (cv_hbm.at[head], kv_ref.at[pl.ds(KROWS + TOK, CROWS), :]),
        ],
        sems,
        4,
    )
    first = jnp.where(ctx_place() == 0, 1.0, 0.0).astype(F32)
    loads[0].wait()
    _, cum_rows, cum_cols = decay_sums(decay_ref)
    finish(packs)
    packs = begin([(kv_ref, payload_hbm), (kv_ref, plane_hbm.at[pl.ds(0, PAY), :])], sems, 8)
    finish(loads[1:])
    finals = []
    for h in range(HEADS_DEV):
        col = cum_cols[:, h : h + 1]
        final = cum_rows[h : h + 1, TOK - 1 : TOK]
        finals.append(final)
        v = v_ref[h]
        keyed_hi, keyed_lo = split2(k_ref[h].astype(F32) * jnp.exp(final - col))
        state = dot(keyed_hi, v, TN) + dot(keyed_lo, v, TN)
        state = state + (first * jnp.exp(final)) * prior_ref[h]
        state_ref[h * HD : (h + 1) * HD, :] = state.astype(BF16)
    state_ref[HEADS_DEV * HD : S_ROWS, :] = decay_lines(finals)
    stores = begin([(state_ref, plane_hbm.at[pl.ds(PAY, S_ROWS), :])], sems, 10)
    finish(packs)
    finish(stores)


def prep(*arrays):
    return run(
        prep_kernel,
        "prep",
        arrays,
        [HBM] * len(arrays),
        [((PAY, HD), BF16, HBM), ((PAY + S_ROWS, HD), BF16, HBM)],
        [
            ((PAY, HD), BF16), (LIN, BF16), (LIN, BF16), ((HEADS_DEV, TOK), F32), (STATE, F32),
            ((S_ROWS, HD), BF16),
        ],
        11,
    )


def roll_kernel(in_hbm, out_hbm, kv_ref, sems):
    z = ctx_place() // N_YC
    loads = begin([(in_hbm.at[(z + 1 + i) % N_Z], kv_ref.at[i]) for i in range(N_Z - 1)], sems)
    stores = []
    for i, load in enumerate(loads):
        load.wait()
        stores += begin([(kv_ref.at[i], out_hbm.at[i])], sems, N_Z - 1 + i)
    finish(stores)


def other_planes(column):
    shape = (N_Z - 1, PAY, HD)
    return run(
        roll_kernel,
        "other_planes",
        (column,),
        [HBM],
        [(shape, BF16, HBM)],
        [(shape, BF16)],
        2 * (N_Z - 1),
    )


def plane_scan_kernel(plane_hbm, own_hbm, own_decay_ref, total_hbm, states, own_ref, total_ref, sems):
    finish(begin([(plane_hbm.at[:, pl.ds(PAY, S_ROWS), :], states)], sems))
    place = ctx_place() % N_YC
    finals = []
    for h in range(HEADS_DEV):
        rows = slice(h * HD, (h + 1) * HD)
        acc = jnp.zeros((HD, HD), F32)
        run = jnp.zeros((1, HD), F32)
        own, own_run = acc, run
        for r in range(N_YC):
            own = jnp.where(place == r, acc, own)
            own_run = jnp.where(place == r, run, own_run)
            decay = decay_of(states[r, HEADS_DEV * HD : S_ROWS, :], h)
            acc = acc * jnp.exp(decay) + states[r, rows, :].astype(F32)
            run = run + decay
        own_ref[h] = own
        own_decay_ref[h : h + 1, :] = own_run
        total_ref[rows, :] = acc.astype(BF16)
        finals.append(run)
    total_ref[HEADS_DEV * HD : S_ROWS, :] = decay_lines(finals)
    first = (ctx_place() % N_CORE) * (HEADS_CORE * HD)
    pairs = [(own_ref, own_hbm)]
    for z in range(N_Z):
        pairs.append((total_ref.at[pl.ds(first, HEADS_CORE * HD), :], total_hbm.at[z, pl.ds(0, HEADS_CORE * HD), :]))
        pairs.append(
            (total_ref.at[pl.ds(HEADS_DEV * HD, D_ROWS), :], total_hbm.at[z, pl.ds(HEADS_CORE * HD, D_ROWS), :])
        )
    finish(begin(pairs, sems, 1))


def plane_scan(plane):
    return run(
        plane_scan_kernel,
        "plane_scan",
        (plane,),
        [HBM],
        [(STATE, F32, HBM), ((HEADS_DEV, HD), F32, VMEM), ((N_Z, U_ROWS, HD), BF16, HBM)],
        [((N_YC, S_ROWS, HD), BF16), (STATE, F32), ((S_ROWS, HD), BF16)],
        2 + 2 * N_Z,
    )


def lightning_mix_kernel(
    q_hbm, mixed_hbm, cum_hbm, own_hbm, own_decay_ref, totals_hbm, prior_hbm,
    out_hbm, square_ref,
    q_ref, mixed_ref, cum_ref, own_ref, totals_ref, prior_ref, out_ref, sems,
):
    loads = begin(
        [
            (totals_hbm, totals_ref), (own_hbm, own_ref), (prior_hbm, prior_ref),
            (cum_hbm, cum_ref), (q_hbm, q_ref), (mixed_hbm, mixed_ref),
        ],
        sems,
    )
    place = ctx_place()
    z_place = place // N_YC
    finish(loads[:3])
    stores = []
    late = loads[3:]
    total = jnp.zeros((TOK, HD), F32)
    for h in range(HEADS_DEV):
        core, inner = h // HEADS_CORE, h % HEADS_CORE
        rows = slice(inner * HD, (inner + 1) * HD)
        acc = jnp.zeros((HD, HD), F32)
        for z in range(N_Z - 1):
            decay = decay_of(totals_ref[core, z, HEADS_CORE * HD : U_ROWS, :], h)
            nxt = acc * jnp.exp(decay) + totals_ref[core, z, rows, :].astype(F32)
            acc = jnp.where(z < z_place, nxt, acc)
        state = own_ref[h] + jnp.exp(own_decay_ref[h : h + 1, :]) * acc
        state = jnp.where(place == 0, prior_ref[h], state)
        hi, low = split2(state)
        if h == 0:
            late[1].wait()
        q = q_ref[h]
        inter = dot(q, hi, NN) + dot(q, low, NN)
        if h == 0:
            late[0].wait()
            late[2].wait()
        mixed = mixed_ref[h] + jnp.exp(cum_ref[:, h : h + 1]) * inter
        out_ref[h] = mixed
        stores += begin([(out_ref.at[h], out_hbm.at[h])], sems, 6 + h)
        total = total + mixed * mixed
    ones = jnp.ones((8, HD), BF16)
    squares = sum(dot(ones, p, NT) for p in split3(total))
    for half in range(TOK // HD):
        line = squares[0:1, half * HD : (half + 1) * HD]
        square_ref[:, half, :] = jnp.broadcast_to(line, (square_ref.shape[0], HD))
    finish(stores)


def lightning_mix(n_tp, *arrays):
    specs = [HBM] * len(arrays)
    specs[4] = VMEM
    return run(
        lightning_mix_kernel,
        "lightning_mix",
        arrays,
        specs,
        [(LIN, F32, HBM), ((n_tp, TOK // HD, HD), F32, VMEM)],
        [
            (LIN, BF16), (LIN, F32), (CUM, F32), (STATE, F32),
            ((N_CORE, N_Z, U_ROWS, HD), BF16), (STATE, F32), (LIN, F32),
        ],
        6 + HEADS_DEV,
    )


def norm_kernel(count, mixed_hbm, squares_ref, gain_hbm, out_hbm, mixed_ref, gain_ref, out_ref, sems):
    loads = begin([(gain_hbm, gain_ref)] + [(mixed_hbm.at[h], mixed_ref.at[h]) for h in range(HEADS_DEV)], sems)
    total = jnp.sum(squares_ref[...], axis=0)
    inv = lax.rsqrt(total * (1.0 / count) + 1e-05)
    t_ids = lax.broadcasted_iota(jnp.int32, (HD, HD), 0)
    s_ids = lax.broadcasted_iota(jnp.int32, (HD, HD), 1)
    factors = []
    for half in range(TOK // HD):
        diag = jnp.where(t_ids == s_ids, jnp.broadcast_to(inv[half : half + 1, :], (HD, HD)), 0.0)
        factors.append(jnp.broadcast_to(jnp.sum(diag, axis=1, keepdims=True), (HD, HD)))
    factor = jnp.concatenate(factors, axis=0)
    loads[0].wait()
    stores = []
    for h in range(HEADS_DEV):
        loads[1 + h].wait()
        out_ref[h] = (mixed_ref[h] * factor * gain_ref[h : h + 1, :]).astype(BF16)
        stores += begin([(out_ref.at[h], out_hbm.at[h])], sems, 1 + HEADS_DEV + h)
    finish(stores)


def lightning_norm(count, mixed, squares, gain):
    return run(
        functools.partial(norm_kernel, float(count)),
        "lightning_norm",
        (mixed, squares, gain),
        [HBM, VMEM, HBM],
        [(LIN, BF16, HBM)],
        [(LIN, F32), ((HEADS_DEV, HD), F32), (LIN, BF16)],
        1 + 2 * HEADS_DEV,
    )


def cache_bias(len_ref, z, r):
    lanes = lax.broadcasted_iota(jnp.int32, (1, CROWS), 1)
    return jnp.where(lanes < len_ref[z * N_YC + r], 0.0, MASK_FILL).astype(F32)


def with_ones(values):
    return jnp.concatenate([values, jnp.ones(values.shape, BF16)], axis=1)


def wide(stat, width):
    return jnp.concatenate([stat] * (width // HD), axis=1)


def by_head(score, soften, fold):
    ahead, held = score(0), None
    for h in range(HEADS_DEV + 1):
        fresh = None
        if h < HEADS_DEV:
            raw = ahead
            if h + 1 < HEADS_DEV:
                ahead = score(h + 1)
            fresh = soften(h, raw)
        if held is not None:
            fold(h - 1, held)
        held = fresh


def near_kernel(
    scale,
    len_ref, q_hbm, plane_hbm, rest_hbm, lq_hbm, lk_hbm, lv_hbm, decay_hbm,
    m_hbm, acc_hbm, mixed_hbm, cum_hbm,
    q_ref, kv, kr, lq_ref, lk_ref, lv_ref, decay_ref, m_ref, acc_ref, mixed_ref, cum_ref, sems,
):
    loads = begin(
        [
            (decay_hbm, decay_ref), (lq_hbm, lq_ref), (lk_hbm, lk_ref), (lv_hbm, lv_ref),
            (q_hbm, q_ref), (plane_hbm.at[:, pl.ds(0, PAY), :], kv), (rest_hbm, kr),
        ],
        sems,
    )
    n_loads = len(loads)
    z = ctx_place() // N_YC
    place = ctx_place() % N_YC
    finish(loads[:4])
    lower, cum_rows, cum_cols = decay_sums(decay_ref)
    cum_ref[...] = cum_cols
    for h in range(HEADS_DEV):
        gap = jnp.where(lower, cum_cols[:, h : h + 1] - cum_rows[h : h + 1, :], 0.0)
        weights = jnp.where(lower, dot(lq_ref[h], lk_ref[h], NT) * jnp.exp(gap), 0.0).astype(BF16)
        mixed_ref[h] = dot(weights, lv_ref[h], NN)
    stores = begin([(mixed_ref, mixed_hbm), (cum_ref, cum_hbm)], sems, n_loads)

    rows = lax.broadcasted_iota(jnp.int32, (TOK, TOK), 0)
    cols = lax.broadcasted_iota(jnp.int32, (TOK, TOK), 1)
    ahead = cols - rows
    bias = [cache_bias(len_ref, z, r) for r in range(N_YC)]
    line = []
    for i in range(N_Z - 1):
        other = (z + 1 + i) % N_Z
        line.append(jnp.full((1, TOK), jnp.where(other < z, 0.0, MASK_FILL).astype(F32)))
        line.append(cache_bias(len_ref, other, place))
    line = jnp.concatenate(line, axis=1)
    finish(loads[4:])
    keys = kv[:, 0:KROWS, :].reshape(N_YC * KROWS, HD)
    values = with_ones(kv[:, KROWS:PAY, :].reshape(N_YC * KROWS, HD))
    column_keys = kr[:, 0:KROWS, :].reshape((N_Z - 1) * KROWS, HD)
    column_values = with_ones(kr[:, KROWS:PAY, :].reshape((N_Z - 1) * KROWS, HD))

    def score(h):
        return dot(q_ref[h], keys, NT), dot(q_ref[h], column_keys, NT)

    def soften(h, raws):
        raw, column_raw = raws
        pieces = []
        for r in range(N_YC):
            span = raw[:, r * KROWS : r * KROWS + TOK]
            pieces.append(jnp.where(ahead <= (place - r) * TOK, span, MASK_FILL))
            pieces.append(raw[:, r * KROWS + TOK : (r + 1) * KROWS] + bias[r])
        raw = jnp.concatenate(pieces, axis=1)
        column_raw = column_raw + line
        peak = jnp.maximum(
            jnp.max(raw, axis=1, keepdims=True), jnp.max(column_raw, axis=1, keepdims=True)
        )
        peak = jnp.broadcast_to(peak, (TOK, HD))
        m_ref[h] = peak
        probs = jnp.exp2((raw - wide(peak, raw.shape[1])) * scale).astype(BF16)
        column_probs = jnp.exp2((column_raw - wide(peak, column_raw.shape[1])) * scale).astype(BF16)
        return probs, column_probs

    def fold(h, probs):
        acc_ref[h] = dot(probs[0], values, NN) + dot(probs[1], column_values, NN)
        stores.extend(
            begin([(m_ref.at[h], m_hbm.at[h]), (acc_ref.at[h], acc_hbm.at[h])], sems, n_loads + 2 + 2 * h)
        )

    by_head(score, soften, fold)
    finish(stores)


SUMS = (HEADS_DEV, TOK, 2 * HD)


def near_work(cache_len, *arrays):
    return run(
        functools.partial(near_kernel, LOG2E / math.sqrt(HD)),
        "near_work",
        (cache_len, *arrays),
        [SMEM] + [HBM] * len(arrays),
        [(LIN, F32, HBM), (SUMS, F32, HBM), (LIN, F32, HBM), (CUM, F32, HBM)],
        [
            (LIN, BF16), ((N_YC, PAY, HD), BF16), ((N_Z - 1, PAY, HD), BF16),
            (LIN, BF16), (LIN, BF16), (LIN, BF16), ((HEADS_DEV, TOK), F32),
            (LIN, F32), (SUMS, F32), (LIN, F32), (CUM, F32),
        ],
        9 + 2 * HEADS_DEV,
    )


def far_kernel(
    scale, len_ref, q_hbm, m_hbm, acc_hbm, kv_hbm, out_hbm, q_ref, m_ref, acc_ref, kv, out_ref, sems
):
    z_place = ctx_place() // N_YC
    place = ctx_place() % N_YC
    others = [(place + 1 + j) % N_YC for j in range(N_FAR)]
    loads = begin([(q_hbm, q_ref), (m_hbm, m_ref), (acc_hbm, acc_ref)], sems)

    def shards(i):
        pairs = [(kv_hbm.at[r, i], kv.at[i, j]) for j, r in enumerate(others)]
        return begin(pairs, sems, 3 + i * N_FAR)

    blocks = [shards(0)]
    finish(loads)
    finish(blocks[0])
    blocks += [shards(i) for i in range(1, N_Z - 1)]

    def update(keys, values, mask):
        def score(h):
            return dot(q_ref[h], keys, NT)

        def soften(h, raw):
            raw = mask(raw)
            m_old = m_ref[h]
            m_new = jnp.maximum(m_old, jnp.max(raw, axis=1, keepdims=True))
            m_ref[h] = m_new
            probs = jnp.exp2((raw - wide(m_new, raw.shape[1])) * scale).astype(BF16)
            return probs, jnp.exp2((m_old - m_new) * scale)

        def fold(h, held):
            probs, alpha = held
            acc_ref[h] = acc_ref[h] * wide(alpha, 2 * HD) + dot(probs, values, NN)

        by_head(score, soften, fold)

    for i in range(N_Z - 1):
        if i > 0:
            finish(blocks[i])
        z = (z_place + 1 + i) % N_Z
        bias = [cache_bias(len_ref, z, r) for r in others]

        @pl.when(z < z_place)
        def whole():
            keys = kv[i, :, 0:KROWS, :].reshape(N_FAR * KROWS, HD)
            values = with_ones(kv[i, :, KROWS:PAY, :].reshape(N_FAR * KROWS, HD))

            def mask(raw):
                pieces = []
                for r in range(N_FAR):
                    pieces.append(raw[:, r * KROWS : r * KROWS + TOK])
                    pieces.append(raw[:, r * KROWS + TOK : (r + 1) * KROWS] + bias[r])
                return jnp.concatenate(pieces, axis=1)

            update(keys, values, mask)

        @pl.when(z > z_place)
        def cache_only():
            keys = kv[i, :, TOK:KROWS, :].reshape(N_FAR * CROWS, HD)
            values = with_ones(kv[i, :, KROWS + TOK : PAY, :].reshape(N_FAR * CROWS, HD))
            line = jnp.concatenate(bias, axis=1)
            update(keys, values, lambda raw: raw + line)

    stores = []
    for h in range(HEADS_DEV):
        acc = acc_ref[h]
        out_ref[h] = (acc[:, 0:HD] / acc[:, HD : 2 * HD]).astype(BF16)
        stores += begin([(out_ref.at[h], out_hbm.at[h])], sems, 3 + (N_Z - 1) * N_FAR + h)
    finish(stores)


def far_attention(cache_len, soft_q, peaks, sums, kv):
    return run(
        functools.partial(far_kernel, LOG2E / math.sqrt(HD)),
        "far_attention",
        (cache_len, soft_q, peaks, sums, kv),
        [SMEM] + [HBM] * 4,
        [(LIN, BF16, HBM)],
        [(LIN, BF16), (LIN, F32), (SUMS, F32), ((N_Z - 1, N_FAR, PAY, HD), BF16), (LIN, BF16)],
        3 + (N_Z - 1) * N_FAR + HEADS_DEV,
    )


def per_device(
    lin_q,
    lin_k,
    lin_v,
    log_decay,
    prior_state,
    lin_gain,
    soft_q,
    span_k,
    span_v,
    cache_k,
    cached_value_rows,
    cache_len,
):
    payload, plane_payload = prep(
        span_k, span_v, cache_k, cached_value_rows, lin_k, lin_v, log_decay, prior_state
    )
    plane = lax.all_gather(plane_payload, "ctx", axis=0, tiled=True, axis_index_groups=YC_GROUPS)
    plane = plane.reshape(N_YC, PAY + S_ROWS, HD)
    column = lax.all_gather(payload, "ctx", axis=0, tiled=True, axis_index_groups=Z_GROUPS)
    rest = other_planes(column.reshape(N_Z, PAY, HD))
    far = lax.all_gather(
        rest.reshape((N_Z - 1) * PAY, HD), "ctx", axis=0, tiled=True, axis_index_groups=YC_GROUPS
    )
    far = far.reshape(N_YC, N_Z - 1, PAY, HD)

    own, own_decay, plane_totals = plane_scan(plane)
    totals = lax.all_to_all(plane_totals, "ctx", 0, 0, axis_index_groups=Z_GROUPS)
    totals = lax.all_gather(totals, "ctx", axis=0, axis_index_groups=CORE_GROUPS)
    peaks, sums, mixed, cum = near_work(
        cache_len, soft_q, plane, rest, lin_q, lin_k, lin_v, log_decay
    )
    own, peaks = lax.optimization_barrier((own, peaks))
    n_tp = lax.axis_size("tp")
    mixed, squares = lightning_mix(
        n_tp, lin_q, mixed, cum, own, own_decay, totals, prior_state
    )
    squares, peaks = lax.optimization_barrier((squares, peaks))
    all_squares = lax.all_to_all(squares, "tp", 0, 0)
    soft_out = far_attention(cache_len, soft_q, peaks, sums, far)
    mixed, soft_out = lax.optimization_barrier((mixed, soft_out))
    normalized = lightning_norm(n_tp * HEADS_DEV * HD, mixed, all_squares, lin_gain)
    return (normalized, soft_out)


def solution(mesh):
    placed = (
        P("tp", "ctx", None),
        P("tp", "ctx", None),
        P("tp", "ctx", None),
        P("tp", "ctx"),
        P("tp", None, None),
        P("tp", None),
        P("tp", "ctx", None),
        P(None, "ctx", None),
        P(None, "ctx", None),
        P(None, "ctx", None),
        P(None, "ctx", None),
        P(),
    )
    return jax.shard_map(
        per_device,
        mesh=mesh,
        in_specs=placed,
        out_specs=(P("tp", "ctx", None), P("tp", "ctx", None)),
        check_vma=False,
    )
```
